32 devices in a mesh: rep: 8 (over y, x, core), own: 4 (over z).
Axes of the slice: x: 2, y: 2, z: 4, core: 2. Of those that a mesh axis runs over, the one named last changes fastest.
Arguments:
- gradients: bfloat16 [8, 4, 4, 256, 256], P('rep', 'own')
- owner_index: int32 [4], replicated, may hold values from 0 to 3, as said below
- left_stats: float32 [8, 256, 256], P('own'), as said below
- right_stats: float32 [8, 256, 256], P('own'), as said below
- left_roots: bfloat16 [8, 256, 256], P('own'), as said below
- right_roots: bfloat16 [8, 256, 256], P('own'), as said below
- first_moment: float32 [8, 256, 256], P('own')
- second_moment: float32 [8, 256, 256], P('own'), may hold values from 0.05 to 5
- master: float32 [8, 256, 256], P('own'), may hold values from -6 to 6
Outputs:
- new_left: float32 [8, 256, 256], P('own')
- new_right: float32 [8, 256, 256], P('own')
- new_first: float32 [8, 256, 256], P('own')
- new_second: float32 [8, 256, 256], P('own')
- weights: bfloat16 [4, 256, 256], P(None, 'rep')
The draws below stay inside these ranges and needn't reach their ends.
Inputs may be any that keep to these rules, and one draw needn't show every extreme that they name: `owner_index`: exactly one owner holds 2 blocks, exactly one holds none, every other holds one. `left_stats`: each matrix is symmetric; every diagonal entry exceeds the sum of the magnitudes of the other entries of its row. `right_stats`: each matrix is symmetric; every diagonal entry exceeds the sum of the magnitudes of the other entries of its row. `left_roots`: each matrix is symmetric. `right_roots`: each matrix is symmetric.
All inputs are finite; a program needn't handle non-finite values.
Results may differ from the reference program's by a relative error of at most 0.001.
Values may be sent and summed in bfloat16 or wider, within the bound.
A program may use at most 64 MiB of HBM per device.

```python
import math
import jax
import jax.numpy as jnp
from jax import lax

BS = 256
CAP = 2
NEWTON = 4
NBLK = 4
SLOTS = 8
N_REP = 8
N_OWN = 4


def log_scales(key, shape):
    return jnp.exp(jax.random.uniform(key, shape, jnp.float32, -1.15, 1.15))


def mirror_upper(values):
    rows_index = jnp.arange(BS, dtype=jnp.int32)[:, None]
    columns_index = jnp.arange(BS, dtype=jnp.int32)[None, :]
    return jnp.where(rows_index < columns_index, values, jnp.swapaxes(values, 1, 2))


def draw_gradients(key, part):
    subkeys = jax.random.split(jax.random.fold_in(key, 3), 3)
    devices = N_REP * N_OWN
    row_scale = log_scales(subkeys[0], (NBLK, BS, 1))
    column_scale = log_scales(subkeys[1], (NBLK, 1, BS))
    values = jax.random.normal(subkeys[2], (N_REP, N_OWN, NBLK, BS, BS), jnp.float32) / math.sqrt(devices)
    return (values * row_scale * column_scale).astype(jnp.bfloat16)


def draw_owner_index(key, part):
    subkeys = jax.random.split(jax.random.fold_in(key, 7), 3)
    base_owner = jax.random.permutation(subkeys[0], N_OWN).astype(jnp.int32)
    heavy = jax.random.randint(subkeys[1], (), 0, N_OWN, dtype=jnp.int32)
    light = (heavy + jax.random.randint(subkeys[2], (), 1, N_OWN, dtype=jnp.int32)) % N_OWN
    return jnp.where(base_owner == light, heavy, base_owner).astype(jnp.int32)


def statistic_draw(key, variant):
    subkeys = jax.random.split(jax.random.fold_in(key, variant), 3)
    count = N_OWN * CAP
    diagonal = jnp.exp(jax.random.uniform(subkeys[0], (count, BS), jnp.float32, math.log(1.0), math.log(3.0)))
    magnitude = jax.random.uniform(subkeys[1], (count, BS, BS), jnp.float32, 0.5, 0.95) / BS
    signs = jnp.where(jax.random.bernoulli(subkeys[2], 0.5, (count, BS, BS)), 1.0, -1.0)
    mirrored = mirror_upper(magnitude * signs)
    identity = jnp.eye(BS, dtype=jnp.float32)
    return identity[None] * diagonal[:, :, None] + (1.0 - identity[None]) * mirrored


def root_draw(key, variant):
    count = N_OWN * CAP
    amplitude = 0.17 / math.sqrt(BS)
    values = jax.random.uniform(jax.random.fold_in(key, variant), (count, BS, BS), jnp.float32, -amplitude, amplitude)
    identity = jnp.eye(BS, dtype=jnp.float32)
    return (identity[None] + (1.0 - identity[None]) * mirror_upper(values)) * 5.0 ** (-0.25)


def draw_left_stats(key, part):
    return statistic_draw(key, 11)


def draw_right_stats(key, part):
    return statistic_draw(key, 12)


def draw_left_roots(key, part):
    return root_draw(key, 21).astype(jnp.bfloat16)


def draw_right_roots(key, part):
    return root_draw(key, 22).astype(jnp.bfloat16)


def draw_first_moment(key, part):
    subkeys = jax.random.split(jax.random.fold_in(key, 31), 3)
    count = N_OWN * CAP
    row_scale = log_scales(subkeys[0], (count, BS, 1))
    column_scale = log_scales(subkeys[1], (count, 1, BS))
    values = jax.random.normal(subkeys[2], (count, BS, BS), jnp.float32)
    return values * row_scale * column_scale


def shard_levels(key, dims, shards, low, high):
    def one(axis_at, shards_of):
        heights = jax.random.uniform(jax.random.fold_in(jax.random.fold_in(key, 6), axis_at), (shards_of,), jnp.float32, low / len(shards), high / len(shards))
        return jnp.repeat(jnp.exp(heights), dims[axis_at] // shards_of).reshape((-1,) + (1,) * (len(dims) - axis_at - 1))

    loudness = one(*shards[0])
    for cut in shards[1:]:
        loudness = loudness * one(*cut)
    return loudness


def centred(own_key, dims, deviation, reach, pieces=(), kind=jnp.bfloat16):
    drawn = deviation * jax.random.normal(own_key, dims, jnp.float32)
    if pieces:
        drawn = drawn * shard_levels(own_key, dims, pieces, -0.22, 0.18)
    return jnp.clip(drawn, -reach, reach).astype(kind)


def setup_inputs(seed: int = 0) -> dict:
    keys = jax.random.split(jax.random.key(seed), 10)
    gradients = draw_gradients(jax.random.fold_in(keys[9], 71), 0)
    owner_index = draw_owner_index(jax.random.fold_in(keys[9], 71), 0)
    left_stats = draw_left_stats(jax.random.fold_in(keys[9], 71), 0)
    right_stats = draw_right_stats(jax.random.fold_in(keys[9], 71), 0)
    left_roots = draw_left_roots(jax.random.fold_in(keys[9], 71), 0)
    right_roots = draw_right_roots(jax.random.fold_in(keys[9], 71), 0)
    first_moment = draw_first_moment(jax.random.fold_in(keys[9], 71), 0)
    second_moment = jnp.clip(jnp.exp(math.log(5.0) - 4.6051702 * jax.random.uniform(keys[7], (SLOTS, BS, BS), jnp.float32) ** shard_levels(keys[7], (SLOTS, BS, BS), ((0, 4),), -0.2, 0.2)), 0.05, 5.0)
    master = centred(keys[8], (SLOTS, BS, BS), 1.0, 6.0, ((0, 4),), jnp.float32)
    return dict(gradients=gradients, owner_index=owner_index, left_stats=left_stats, right_stats=right_stats, left_roots=left_roots, right_roots=right_roots, first_moment=first_moment, second_moment=second_moment, master=master)


stat_decay = 0.95
first_decay = 0.9
second_decay = 0.99
learning_rate = 0.5

def product(first_factor, second_factor):
    return jnp.matmul(first_factor, second_factor, precision=lax.Precision.HIGHEST)

def destinations(owner_index, capacity):
    block_count = owner_index.shape[0]
    positions = jnp.arange(block_count, dtype=jnp.int32)
    same_owner = owner_index[:, None] == owner_index[None, :]
    earlier = positions[None, :] < positions[:, None]
    ranking = lax.optimization_barrier(jnp.sum((same_owner & earlier).astype(jnp.int32), axis=1)).astype(jnp.int32)
    return (owner_index.astype(jnp.int32) * capacity + ranking).astype(jnp.int32)

def inverse_root(statistic, initial):
    current = initial
    for iteration in range(NEWTON):
        square = product(current, current)
        fourth = product(square, square)
        residual = product(fourth, statistic)
        current = (5.0 * current - product(current, residual)) / 4.0
    return current

def reference(gradients, owner_index, left_stats, right_stats, left_roots, right_roots, first_moment, second_moment, master):
    destination = destinations(owner_index, CAP)
    summed = lax.optimization_barrier(jnp.sum(gradients, axis=(0, 1), dtype=jnp.float32))
    transposed = jnp.swapaxes(summed, 1, 2)
    left_new = stat_decay * left_stats[destination] + (1.0 - stat_decay) / BS * product(summed, transposed)
    right_new = stat_decay * right_stats[destination] + (1.0 - stat_decay) / BS * product(transposed, summed)
    left_root = inverse_root(left_new, left_roots[destination].astype(jnp.float32))
    right_root = inverse_root(right_new, right_roots[destination].astype(jnp.float32))
    first_new = first_decay * first_moment[destination] + (1.0 - first_decay) * summed
    second_new = second_decay * second_moment[destination] + (1.0 - second_decay) * summed * summed
    adam_step = first_new / (jnp.sqrt(second_new) + 1e-08)
    precond = product(product(left_root, summed), right_root)
    graft = jnp.sqrt(lax.optimization_barrier(jnp.sum(adam_step * adam_step, axis=(1, 2)))) / (jnp.sqrt(lax.optimization_barrier(jnp.sum(precond * precond, axis=(1, 2)))) + 1e-06)
    weights = (master[destination] - learning_rate * graft[:, None, None] * precond).astype(jnp.bfloat16)
    new_left = left_stats.at[destination].set(left_new)
    new_right = right_stats.at[destination].set(right_new)
    new_first = first_moment.at[destination].set(first_new)
    new_second = second_moment.at[destination].set(second_new)
    return (new_left, new_right, new_first, new_second, weights)
```

```python
import functools

import jax
import jax.numpy as jnp
from jax import lax
from jax.experimental import pallas as pl
from jax.experimental.pallas import tpu as pltpu
from jax.sharding import PartitionSpec as P

NEWTON = 4
VMEM_UNITS = 246


stat_decay = 0.95
first_decay = 0.9
second_decay = 0.99
learning_rate = 0.5


def slot_of(owner_ref, block, capacity):
    rank = jnp.int32(0)
    for earlier in range(block):
        rank = rank + jnp.where(owner_ref[earlier] == owner_ref[block], 1, 0)
    return owner_ref[block] * capacity + rank


def send(source, target, send_sem, recv_sem, device):
    copy = pltpu.make_async_remote_copy(
        src_ref=source,
        dst_ref=target,
        send_sem=send_sem,
        recv_sem=recv_sem,
        device_id=device,
        device_id_type=pl.DeviceIdType.MESH,
    )
    copy.start()
    return copy


def greet(devices):
    barrier = pltpu.get_barrier_semaphore()
    for device in devices:
        pl.semaphore_signal(
            barrier, inc=1, device_id=device, device_id_type=pl.DeviceIdType.MESH
        )
    pl.semaphore_wait(barrier, len(devices))


def dot(first, second, first_axis=1, second_axis=0):
    return lax.dot_general(
        first,
        second,
        (((first_axis,), (second_axis,)), ((), ())),
        preferred_element_type=jnp.float32,
    )


def parts(value):
    upper = value.astype(jnp.bfloat16)
    lower = (value - upper.astype(jnp.float32)).astype(jnp.bfloat16)
    return upper, lower


def multiply(first, second, first_axis=1, second_axis=0):
    return dot(first[0], second[0], first_axis, second_axis) + (
        dot(first[0], second[1], first_axis, second_axis)
        + dot(first[1], second[0], first_axis, second_axis)
    )


def total(value):
    return jnp.sum(jnp.sum(value, axis=0, keepdims=True), axis=1, keepdims=True)


def step_kernel(
    reps,
    owns,
    chunks,
    owner_ref,
    gradients_ref,
    left_ref,
    right_ref,
    left_root_ref,
    right_root_ref,
    first_ref,
    second_ref,
    master_ref,
    new_left_ref,
    new_right_ref,
    new_first_ref,
    new_second_ref,
    weights_ref,
    raw,
    partial,
    arrived,
    piece_sum,
    summed,
    other,
    roots,
    left_in,
    right_in,
    first_in,
    second_in,
    master_in,
    fifth,
    upper,
    lower,
    current,
    kept,
    outgoing,
    gathered,
    load_sem,
    mine_sem,
    raw_send,
    raw_recv,
    own_send,
    own_recv,
    sum_send,
    sum_recv,
    other_send,
    other_recv,
    row_send,
    row_recv,
):
    rep = lax.axis_index("rep")
    own = lax.axis_index("own")
    block_count = owner_ref.shape[0]
    capacity = new_left_ref.shape[0]
    block_size = new_left_ref.shape[-1]
    row_count = weights_ref.shape[1]
    piece_rows = row_count // chunks
    groups = reps // capacity
    high = lax.div(rep, capacity)
    low = lax.rem(rep, capacity)
    sides = range(2)

    def rep_device(target):
        return (target, own)

    def own_device(target):
        return (rep, target)

    pair_rows = pl.ds(
        pl.multiple_of(high * capacity * row_count, capacity * row_count), capacity * row_count
    )
    mine = []
    for chunk in range(chunks):
        mine.append(
            pltpu.make_async_copy(
                gradients_ref.at[:, rep * chunks + chunk], raw[chunk].at[0], mine_sem.at[chunk]
            )
        )
        mine[-1].start()
    greet(
        [own_device(lax.rem(own + step, owns)) for step in range(1, owns)]
        + [rep_device(lax.rem(rep + step, reps)) for step in range(1, reps)]
    )
    raw_copies = []
    for chunk in range(chunks):
        raw_copies.append([])
        for step in range(1, reps):
            target = lax.rem(rep + step, reps)
            raw_copies[-1].append(
                send(
                    gradients_ref.at[:, target * chunks + chunk],
                    raw[chunk].at[step],
                    raw_send.at[chunk, step],
                    raw_recv.at[chunk, step],
                    rep_device(target),
                )
            )
    loads = []
    for place, (source_ref, target_ref) in enumerate(
        (
            (left_root_ref.at[low], roots.at[0]),
            (right_root_ref.at[low], roots.at[1]),
            (left_ref, left_in),
            (right_ref, right_in),
            (first_ref, first_in),
            (second_ref, second_in),
            (master_ref.at[low, pair_rows, :], master_in),
        )
    ):
        loads.append(pltpu.make_async_copy(source_ref, target_ref, load_sem.at[place]))
        loads[-1].start()
    slots = [slot_of(owner_ref, block, capacity) for block in range(block_count)]

    def source(slot):
        found = jnp.int32(0)
        for block in range(block_count):
            found = found + jnp.where(slots[block] == slot, block, 0)
        return found

    loads[0].wait()
    loads[1].wait()
    squares = [parts(dot(roots[side], roots[side])) for side in sides]
    fourths = [parts(multiply(squares[side], squares[side])) for side in sides]
    for side in sides:
        fifth[side] = dot(roots[side], fourths[side][0]) + dot(roots[side], fourths[side][1])

    own_copies = []
    for chunk in range(chunks):
        mine[chunk].wait()
        for copy in raw_copies[chunk]:
            copy.wait_recv()
        own_copies.append([])
        for step in [*range(1, owns), 0]:
            target = lax.rem(own + step, owns)
            for place in range(capacity):
                block = source(target * capacity + place)
                value = raw[chunk][0, block].astype(jnp.float32)
                for peer in range(1, reps):
                    value = value + raw[chunk][peer, block].astype(jnp.float32)
                partial[chunk, step, place] = value
            if step:
                own_copies[-1].append(
                    send(
                        partial.at[chunk, step],
                        arrived.at[chunk, step],
                        own_send.at[chunk, step],
                        own_recv.at[chunk, step],
                        own_device(target),
                    )
                )

    sum_copies = []
    for chunk in range(chunks):
        for copy in own_copies[chunk]:
            copy.wait_recv()
        value = partial[chunk, 0]
        for step in range(1, owns):
            value = value + arrived[chunk, step]
        piece_sum[chunk] = value
        start = pl.multiple_of(rep * row_count + chunk * piece_rows, piece_rows)
        rows = pl.ds(start, piece_rows)
        for step in range(1, reps):
            target = lax.rem(rep + step, reps)
            sum_copies.append(
                send(
                    piece_sum.at[chunk, lax.rem(target, capacity)],
                    summed.at[rows, :],
                    sum_send.at[chunk, step],
                    sum_recv.at[chunk, step],
                    rep_device(target),
                )
            )
        summed[rows, :] = piece_sum[chunk, low]
    for copy in loads[2:]:
        copy.wait()
    for copy in sum_copies:
        copy.wait_recv()
    others = [
        send(
            summed,
            other.at[step],
            other_send.at[step],
            other_recv.at[step],
            rep_device(high * capacity + lax.rem(low + step, capacity)),
        )
        for step in range(1, capacity)
    ]

    scale = (1.0 - stat_decay) / block_size

    def occupied(place):
        count = jnp.int32(0)
        for block in range(block_count):
            count = count + jnp.where(slots[block] == own * capacity + place, 1, 0)
        return count > 0

    def moments(place, gradient, held):
        first_new = first_decay * first_in[place] + (1.0 - first_decay) * gradient
        second_new = (
            second_decay * second_in[place] + (1.0 - second_decay) * gradient * gradient
        )
        new_first_ref[place] = jnp.where(held, first_new, first_in[place])
        new_second_ref[place] = jnp.where(held, second_new, second_in[place])
        return first_new, second_new

    def statistics(place, split, held):
        left = stat_decay * left_in[place] + scale * multiply(split, split, 1, 1)
        right = stat_decay * right_in[place] + scale * multiply(split, split, 0, 0)
        new_left_ref[place] = jnp.where(held, left, left_in[place])
        new_right_ref[place] = jnp.where(held, right, right_in[place])
        return left, right

    held = occupied(low)
    gradient = summed[...]
    for side, value in enumerate(statistics(low, parts(gradient), held)):
        upper[side], lower[side] = parts(value)

    def statistic(side):
        return upper[side], lower[side]

    for side in sides:
        current[side] = (
            5.0 * roots[side].astype(jnp.float32)
            - multiply(parts(fifth[side]), statistic(side))
        ) / 4.0
    first_new, second_new = moments(low, gradient, held)
    adam_step = first_new / (jnp.sqrt(second_new) + 1e-08)
    adam_norm = jnp.sqrt(total(adam_step * adam_step))

    def newton(iteration, carry):
        split = [parts(current[side]) for side in sides]
        squares = [parts(multiply(split[side], split[side])) for side in sides]
        cubes = [parts(multiply(split[side], squares[side])) for side in sides]
        rests = [parts(multiply(squares[side], statistic(side))) for side in sides]
        for side in sides:
            current[side] = (5.0 * current[side] - multiply(cubes[side], rests[side])) / 4.0
        return carry

    lax.fori_loop(1, NEWTON, newton, 0)

    halfway = multiply(parts(current[0]), parts(summed[...]))
    precond = multiply(parts(halfway), parts(current[1]))
    graft = adam_norm / (jnp.sqrt(total(precond * precond)) + 1e-06)
    kept[...] = precond
    weight = (master_in[...] - learning_rate * graft * kept[pair_rows, :]).astype(jnp.bfloat16)
    row_copies = []
    for member in range(capacity):
        outgoing[member] = weight[member * row_count : (member + 1) * row_count]
    for step in [*range(1, owns), 0]:
        for shift in range(capacity):
            if step or shift:
                member = lax.rem(low + shift, capacity)
                row_copies.append(
                    send(
                        outgoing.at[member],
                        gathered.at[step, low],
                        row_send.at[step, shift],
                        row_recv.at[step, shift],
                        (high * capacity + member, lax.rem(own + step, owns)),
                    )
                )
    gathered[0, low] = outgoing[low]

    for step in range(1, capacity):
        others[step - 1].wait_recv()
        place = lax.rem(low + capacity - step, capacity)
        gradient = other[step]
        held = occupied(place)
        statistics(place, parts(gradient), held)
        moments(place, gradient, held)
    for copy in [copy for copies in raw_copies + own_copies for copy in copies]:
        copy.wait_send()
    for copy in sum_copies + others + row_copies:
        copy.wait_send()
    for copy in row_copies:
        copy.wait_recv()
    for block in range(block_count):
        step = lax.rem(own + owns - owner_ref[block], owns)
        place = jnp.minimum(slots[block] - owner_ref[block] * capacity, capacity - 1)
        weights_ref[block] = gathered[step, place]


def write(*refs):
    count = (len(refs) - 1) // 2
    stores = []
    for index in range(count):
        source_ref, target_ref = refs[index], refs[count + index]
        stores.append(pltpu.make_async_copy(source_ref, target_ref, refs[-1].at[index]))
        stores[-1].start()
    for store in stores:
        store.wait()


def local(
    reps,
    owns,
    gradients,
    owner_index,
    left_stats,
    right_stats,
    left_roots,
    right_roots,
    first_moment,
    second_moment,
    master,
):
    capacity = left_stats.shape[0]
    block_size = left_stats.shape[-1]
    block_count = owner_index.shape[0]
    row_count = block_size // reps
    chunks = 4 if row_count % 32 == 0 else 1
    piece_rows = row_count // chunks
    vmem = pl.BlockSpec(memory_space=pltpu.VMEM)
    smem = pl.BlockSpec(memory_space=pltpu.SMEM)
    hbm = pl.BlockSpec(memory_space=pltpu.HBM)
    dma = pltpu.SemaphoreType.DMA
    square = (block_size, block_size)
    piece = (capacity, piece_rows, block_size)
    whole = (capacity, *square)
    double = (2, *square)
    shapes = [(whole, jnp.float32)] * 4 + [((block_count, row_count, block_size), jnp.bfloat16)]

    results = pl.pallas_call(
        functools.partial(step_kernel, reps, owns, chunks),
        out_shape=[pltpu.VMEM(*leaf) for leaf in shapes],
        in_specs=[smem] + [hbm] * 8,
        out_specs=[vmem] * 5,
        scratch_shapes=[
            (pltpu.VMEM((reps, block_count, piece_rows, block_size), jnp.bfloat16),) * chunks,
            pltpu.VMEM((chunks, owns, *piece), jnp.float32),
            pltpu.VMEM((chunks, owns, *piece), jnp.float32),
            pltpu.VMEM((chunks, *piece), jnp.float32),
            pltpu.VMEM(square, jnp.float32),
            pltpu.VMEM(whole, jnp.float32),
            pltpu.VMEM(double, jnp.bfloat16),
            pltpu.VMEM(whole, jnp.float32),
            pltpu.VMEM(whole, jnp.float32),
            pltpu.VMEM(whole, jnp.float32),
            pltpu.VMEM(whole, jnp.float32),
            pltpu.VMEM((capacity * row_count, block_size), jnp.float32),
            pltpu.VMEM(double, jnp.float32),
            pltpu.VMEM(double, jnp.bfloat16),
            pltpu.VMEM(double, jnp.bfloat16),
            pltpu.VMEM(double, jnp.float32),
            pltpu.VMEM(square, jnp.float32),
            pltpu.VMEM((capacity, row_count, block_size), jnp.bfloat16),
            pltpu.VMEM((owns, capacity, row_count, block_size), jnp.bfloat16),
            dma((7,)),
            dma((chunks,)),
            dma((chunks, reps)),
            dma((chunks, reps)),
            dma((chunks, owns)),
            dma((chunks, owns)),
            dma((chunks, reps)),
            dma((chunks, reps)),
            dma((capacity,)),
            dma((capacity,)),
            dma((owns, capacity)),
            dma((owns, capacity)),
        ],
        compiler_params=pltpu.CompilerParams(
            collective_id=0, has_side_effects=True, vmem_limit_bytes=VMEM_UNITS * 2**18
        ),
        name="step",
    )(
        owner_index,
        gradients.reshape(block_count, reps * chunks, piece_rows, block_size),
        left_stats,
        right_stats,
        left_roots,
        right_roots,
        first_moment,
        second_moment,
        master,
    )
    return tuple(
        pl.pallas_call(
            write,
            out_shape=[jax.ShapeDtypeStruct(*leaf) for leaf in shapes],
            in_specs=[vmem] * 5,
            out_specs=[hbm] * 5,
            scratch_shapes=[dma((5,))],
            compiler_params=pltpu.CompilerParams(vmem_limit_bytes=VMEM_UNITS * 2**18),
            name="write",
        )(*[pltpu.with_memory_space_constraint(leaf, pltpu.VMEM) for leaf in results])
    )


def solution(mesh):
    return jax.shard_map(
        functools.partial(local, mesh.shape["rep"], mesh.shape["own"]),
        mesh=mesh,
        in_specs=(
            P("rep", "own", None, None, None),
            P(),
            P("own", None, None),
            P("own", None, None),
            P("own", None, None),
            P("own", None, None),
            P("own", None, None),
            P("own", None, None),
            P("own", None, None),
        ),
        out_specs=(
            P("own", None, None),
            P("own", None, None),
            P("own", None, None),
            P("own", None, None),
            P(None, "rep", None),
        ),
        check_vma=False,
    )
```

```python
import functools

import jax
import jax.numpy as jnp
from jax import lax
from jax.experimental import pallas as pl
from jax.experimental.pallas import tpu as pltpu
from jax.sharding import PartitionSpec as P

NEWTON = 4
VMEM_UNITS = 246


stat_decay = 0.95
first_decay = 0.9
second_decay = 0.99
learning_rate = 0.5


def slot_of(owner_ref, block, capacity):
    rank = jnp.int32(0)
    for earlier in range(block):
        rank = rank + jnp.where(owner_ref[earlier] == owner_ref[block], 1, 0)
    return owner_ref[block] * capacity + rank


def send(source, target, send_sem, recv_sem, device):
    copy = pltpu.make_async_remote_copy(
        src_ref=source,
        dst_ref=target,
        send_sem=send_sem,
        recv_sem=recv_sem,
        device_id=device,
        device_id_type=pl.DeviceIdType.MESH,
    )
    copy.start()
    return copy


def greet(devices):
    barrier = pltpu.get_barrier_semaphore()
    for device in devices:
        pl.semaphore_signal(
            barrier, inc=1, device_id=device, device_id_type=pl.DeviceIdType.MESH
        )
    pl.semaphore_wait(barrier, len(devices))


def dot(first, second, first_axis=1, second_axis=0):
    return lax.dot_general(
        first,
        second,
        (((first_axis,), (second_axis,)), ((), ())),
        preferred_element_type=jnp.float32,
    )


def parts(value):
    upper = value.astype(jnp.bfloat16)
    lower = (value - upper.astype(jnp.float32)).astype(jnp.bfloat16)
    return upper, lower


def multiply(first, second, first_axis=1, second_axis=0):
    half = first[0].shape[1 - first_axis] // 2
    halves = []
    for rows in (slice(0, half), slice(half, 2 * half)):
        upper, lower = [
            part[rows] if first_axis else part[:, rows] for part in first
        ]
        halves.append(
            dot(upper, second[0], first_axis, second_axis)
            + (
                dot(upper, second[1], first_axis, second_axis)
                + dot(lower, second[0], first_axis, second_axis)
            )
        )
    return jnp.concatenate(halves, axis=0)


def total(value):
    return jnp.sum(jnp.sum(value, axis=0, keepdims=True), axis=1, keepdims=True)


def step_kernel(
    reps,
    owns,
    chunks,
    owner_in,
    gradients_ref,
    left_ref,
    right_ref,
    left_root_ref,
    right_root_ref,
    first_ref,
    second_ref,
    master_ref,
    new_left_ref,
    new_right_ref,
    new_first_ref,
    new_second_ref,
    weights_ref,
    owner_ref,
    staged,
    raw,
    partial,
    arrived,
    piece_sum,
    summed,
    other,
    roots,
    left_in,
    right_in,
    first_in,
    second_in,
    master_in,
    fifth,
    upper,
    lower,
    current,
    kept,
    outgoing,
    gathered,
    load_sem,
    mine_sem,
    raw_send,
    raw_recv,
    own_send,
    own_recv,
    sum_send,
    sum_recv,
    other_send,
    other_recv,
    row_send,
    row_recv,
):
    rep = lax.axis_index("rep")
    own = lax.axis_index("own")
    block_count = owner_ref.shape[0]
    capacity = new_left_ref.shape[0]
    block_size = new_left_ref.shape[-1]
    row_count = weights_ref.shape[1]
    piece_rows = row_count // chunks
    groups = reps // capacity
    high = lax.div(rep, capacity)
    low = lax.rem(rep, capacity)
    sides = range(2)

    def rep_device(target):
        return (target, own)

    def own_device(target):
        return (rep, target)

    pair_rows = pl.ds(
        pl.multiple_of(high * capacity * row_count, capacity * row_count), capacity * row_count
    )
    mine = pltpu.make_async_copy(gradients_ref, staged, mine_sem.at[0])
    mine.start()
    owners = pltpu.make_async_copy(owner_in, owner_ref, mine_sem.at[1])
    owners.start()
    greet(
        [own_device(lax.rem(own + step, owns)) for step in range(1, owns)]
        + [rep_device(lax.rem(rep + step, reps)) for step in range(1, reps)]
    )
    mine.wait()
    def far(turn):
        down = owns - 1 - turn
        down = down - jnp.where(down <= own, 1, 0)
        up = turn + jnp.where(turn >= own, 1, 0)
        return jnp.where(own < owns // 2, down, up)

    raw_copies = []
    for chunk in range(chunks):
        raw_copies.append([])
        for step in range(1, reps):
            target = lax.rem(rep + step, reps)
            raw_copies[-1].append(
                send(
                    staged.at[:, target * chunks + chunk],
                    raw[chunk].at[step],
                    raw_send.at[chunk, step],
                    raw_recv.at[chunk, step],
                    rep_device(target),
                )
            )
    loads = []
    for place, (source_ref, target_ref) in enumerate(
        (
            (left_root_ref.at[low], roots.at[0]),
            (right_root_ref.at[low], roots.at[1]),
            (left_ref, left_in),
            (right_ref, right_in),
            (first_ref, first_in),
            (second_ref, second_in),
            (master_ref.at[low, pair_rows, :], master_in),
        )
    ):
        loads.append(pltpu.make_async_copy(source_ref, target_ref, load_sem.at[place]))
        loads[-1].start()
    owners.wait()
    slots = [slot_of(owner_ref, block, capacity) for block in range(block_count)]

    def source(slot):
        found = jnp.int32(0)
        for block in range(block_count):
            found = found + jnp.where(slots[block] == slot, block, 0)
        return found

    loads[0].wait()
    loads[1].wait()
    squares = [parts(dot(roots[side], roots[side])) for side in sides]
    fourths = [parts(multiply(squares[side], squares[side])) for side in sides]
    for side in sides:
        fifth[side] = dot(roots[side], fourths[side][0]) + dot(roots[side], fourths[side][1])

    own_copies = []
    for chunk in range(chunks):
        for copy in raw_copies[chunk]:
            copy.wait_recv()
        own_copies.append([])
        for turn in range(owns):
            target = far(turn) if turn < owns - 1 else own
            step = lax.rem(target - own + owns, owns) if turn < owns - 1 else 0
            for place in range(capacity):
                block = source(target * capacity + place)
                value = staged[block, rep * chunks + chunk].astype(jnp.float32)
                for peer in range(1, reps):
                    value = value + raw[chunk][peer, block].astype(jnp.float32)
                partial[chunk, step, place] = value
            if turn < owns - 1:
                own_copies[-1].append(
                    send(
                        partial.at[chunk, step],
                        arrived.at[chunk, step],
                        own_send.at[chunk, step],
                        own_recv.at[chunk, step],
                        own_device(target),
                    )
                )

    sum_copies = []
    for chunk in range(chunks):
        for copy in own_copies[chunk]:
            copy.wait_recv()
        value = partial[chunk, 0]
        for step in range(1, owns):
            value = value + arrived[chunk, step]
        piece_sum[chunk] = value
        start = pl.multiple_of(rep * row_count + chunk * piece_rows, piece_rows)
        rows = pl.ds(start, piece_rows)
        for step in range(1, reps):
            target = lax.rem(rep + step, reps)
            sum_copies.append(
                send(
                    piece_sum.at[chunk, lax.rem(target, capacity)],
                    summed.at[rows, :],
                    sum_send.at[chunk, step],
                    sum_recv.at[chunk, step],
                    rep_device(target),
                )
            )
        summed[rows, :] = piece_sum[chunk, low]
    for copy in loads[2:]:
        copy.wait()
    for copy in sum_copies:
        copy.wait_recv()
    others = [
        send(
            summed,
            other.at[step],
            other_send.at[step],
            other_recv.at[step],
            rep_device(high * capacity + lax.rem(low + step, capacity)),
        )
        for step in range(1, capacity)
    ]

    scale = (1.0 - stat_decay) / block_size

    def occupied(place):
        count = jnp.int32(0)
        for block in range(block_count):
            count = count + jnp.where(slots[block] == own * capacity + place, 1, 0)
        return count > 0

    def moments(place, gradient, held):
        first_new = first_decay * first_in[place] + (1.0 - first_decay) * gradient
        second_new = (
            second_decay * second_in[place] + (1.0 - second_decay) * gradient * gradient
        )
        new_first_ref[place] = jnp.where(held, first_new, first_in[place])
        new_second_ref[place] = jnp.where(held, second_new, second_in[place])
        return first_new, second_new

    def statistics(place, split, held):
        left = stat_decay * left_in[place] + scale * multiply(split, split, 1, 1)
        right = stat_decay * right_in[place] + scale * multiply(split, split, 0, 0)
        new_left_ref[place] = jnp.where(held, left, left_in[place])
        new_right_ref[place] = jnp.where(held, right, right_in[place])
        return left, right

    held = occupied(low)
    gradient = summed[...]
    for side, value in enumerate(statistics(low, parts(gradient), held)):
        upper[side], lower[side] = parts(value)

    def statistic(side):
        return upper[side], lower[side]

    for side in sides:
        current[side] = (
            5.0 * roots[side].astype(jnp.float32)
            - multiply(parts(fifth[side]), statistic(side))
        ) / 4.0
    first_new, second_new = moments(low, gradient, held)
    adam_step = first_new / (jnp.sqrt(second_new) + 1e-08)
    adam_norm = jnp.sqrt(total(adam_step * adam_step))

    def newton(iteration, carry):
        split = [parts(current[side]) for side in sides]
        squares = [parts(multiply(split[side], split[side])) for side in sides]
        rests = [parts(multiply(squares[side], statistic(side))) for side in sides]
        cubes = [parts(multiply(split[side], squares[side])) for side in sides]
        for side in sides:
            current[side] = (5.0 * current[side] - multiply(cubes[side], rests[side])) / 4.0
        return carry

    lax.fori_loop(1, NEWTON, newton, 0)

    halfway = multiply(parts(current[0]), parts(summed[...]))
    precond = multiply(parts(halfway), parts(current[1]))
    graft = adam_norm / (jnp.sqrt(total(precond * precond)) + 1e-06)
    kept[...] = precond
    weight = (master_in[...] - learning_rate * graft * kept[pair_rows, :]).astype(jnp.bfloat16)
    row_copies = []
    for member in range(capacity):
        outgoing[member] = weight[member * row_count : (member + 1) * row_count]
    for turn in range(owns):
        target = far(turn) if turn < owns - 1 else own
        step = lax.rem(target - own + owns, owns) if turn < owns - 1 else 0
        for shift in range(capacity):
            if turn < owns - 1 or shift:
                member = lax.rem(low + shift, capacity)
                row_copies.append(
                    send(
                        outgoing.at[member],
                        gathered.at[step, low],
                        row_send.at[step, shift],
                        row_recv.at[step, shift],
                        (high * capacity + member, target),
                    )
                )
    gathered[0, low] = outgoing[low]

    for step in range(1, capacity):
        others[step - 1].wait_recv()
        place = lax.rem(low + capacity - step, capacity)
        gradient = other[step]
        held = occupied(place)
        statistics(place, parts(gradient), held)
        moments(place, gradient, held)
    for copy in [copy for copies in raw_copies + own_copies for copy in copies]:
        copy.wait_send()
    for copy in sum_copies + others + row_copies:
        copy.wait_send()
    for copy in row_copies:
        copy.wait_recv()
    for block in range(block_count):
        step = lax.rem(own + owns - owner_ref[block], owns)
        place = jnp.minimum(slots[block] - owner_ref[block] * capacity, capacity - 1)
        weights_ref[block] = gathered[step, place]


def write(*refs):
    count = (len(refs) - 1) // 2
    stores = []
    for index in range(count):
        source_ref, target_ref = refs[index], refs[count + index]
        stores.append(pltpu.make_async_copy(source_ref, target_ref, refs[-1].at[index]))
        stores[-1].start()
    for store in stores:
        store.wait()


def local(
    reps,
    owns,
    gradients,
    owner_index,
    left_stats,
    right_stats,
    left_roots,
    right_roots,
    first_moment,
    second_moment,
    master,
):
    capacity = left_stats.shape[0]
    block_size = left_stats.shape[-1]
    block_count = owner_index.shape[0]
    row_count = block_size // reps
    chunks = 4 if row_count % 32 == 0 else 1
    piece_rows = row_count // chunks
    vmem = pl.BlockSpec(memory_space=pltpu.VMEM)
    hbm = pl.BlockSpec(memory_space=pltpu.HBM)
    dma = pltpu.SemaphoreType.DMA
    square = (block_size, block_size)
    piece = (capacity, piece_rows, block_size)
    whole = (capacity, *square)
    double = (2, *square)
    shapes = [(whole, jnp.float32)] * 4 + [((block_count, row_count, block_size), jnp.bfloat16)]

    results = pl.pallas_call(
        functools.partial(step_kernel, reps, owns, chunks),
        out_shape=[pltpu.VMEM(*leaf) for leaf in shapes],
        in_specs=[hbm] * 9,
        out_specs=[vmem] * 5,
        scratch_shapes=[
            pltpu.SMEM((block_count,), jnp.int32),
            pltpu.VMEM((block_count, reps * chunks, piece_rows, block_size), jnp.bfloat16),
            (pltpu.VMEM((reps, block_count, piece_rows, block_size), jnp.bfloat16),) * chunks,
            pltpu.VMEM((chunks, owns, *piece), jnp.float32),
            pltpu.VMEM((chunks, owns, *piece), jnp.float32),
            pltpu.VMEM((chunks, *piece), jnp.float32),
            pltpu.VMEM(square, jnp.float32),
            pltpu.VMEM(whole, jnp.float32),
            pltpu.VMEM(double, jnp.bfloat16),
            pltpu.VMEM(whole, jnp.float32),
            pltpu.VMEM(whole, jnp.float32),
            pltpu.VMEM(whole, jnp.float32),
            pltpu.VMEM(whole, jnp.float32),
            pltpu.VMEM((capacity * row_count, block_size), jnp.float32),
            pltpu.VMEM(double, jnp.float32),
            pltpu.VMEM(double, jnp.bfloat16),
            pltpu.VMEM(double, jnp.bfloat16),
            pltpu.VMEM(double, jnp.float32),
            pltpu.VMEM(square, jnp.float32),
            pltpu.VMEM((capacity, row_count, block_size), jnp.bfloat16),
            pltpu.VMEM((owns, capacity, row_count, block_size), jnp.bfloat16),
            dma((7,)),
            dma((2,)),
            dma((chunks, reps)),
            dma((chunks, reps)),
            dma((chunks, owns)),
            dma((chunks, owns)),
            dma((chunks, reps)),
            dma((chunks, reps)),
            dma((capacity,)),
            dma((capacity,)),
            dma((owns, capacity)),
            dma((owns, capacity)),
        ],
        compiler_params=pltpu.CompilerParams(
            collective_id=0, has_side_effects=True, vmem_limit_bytes=VMEM_UNITS * 2**18
        ),
        name="step",
    )(
        owner_index,
        gradients.reshape(block_count, reps * chunks, piece_rows, block_size),
        left_stats,
        right_stats,
        left_roots,
        right_roots,
        first_moment,
        second_moment,
        master,
    )
    return tuple(
        pl.pallas_call(
            write,
            out_shape=[jax.ShapeDtypeStruct(*leaf) for leaf in shapes],
            in_specs=[vmem] * 5,
            out_specs=[hbm] * 5,
            scratch_shapes=[dma((5,))],
            compiler_params=pltpu.CompilerParams(vmem_limit_bytes=VMEM_UNITS * 2**18),
            name="write",
        )(*[pltpu.with_memory_space_constraint(leaf, pltpu.VMEM) for leaf in results])
    )


def solution(mesh):
    return jax.shard_map(
        functools.partial(local, mesh.shape["rep"], mesh.shape["own"]),
        mesh=mesh,
        in_specs=(
            P("rep", "own", None, None, None),
            P(),
            P("own", None, None),
            P("own", None, None),
            P("own", None, None),
            P("own", None, None),
            P("own", None, None),
            P("own", None, None),
            P("own", None, None),
        ),
        out_specs=(
            P("own", None, None),
            P("own", None, None),
            P("own", None, None),
            P("own", None, None),
            P(None, "rep", None),
        ),
        check_vma=False,
    )
```

```python
import functools

import jax
import jax.numpy as jnp
from jax import lax
from jax.experimental import pallas as pl
from jax.experimental.pallas import tpu as pltpu
from jax.sharding import PartitionSpec as P

NEWTON = 4
VMEM_UNITS = 246


stat_decay = 0.95
first_decay = 0.9
second_decay = 0.99
learning_rate = 0.5


def slot_of(owner_ref, block, capacity):
    rank = jnp.int32(0)
    for earlier in range(block):
        rank = rank + jnp.where(owner_ref[earlier] == owner_ref[block], 1, 0)
    return owner_ref[block] * capacity + rank


def send(source, target, send_sem, recv_sem, device):
    copy = pltpu.make_async_remote_copy(
        src_ref=source,
        dst_ref=target,
        send_sem=send_sem,
        recv_sem=recv_sem,
        device_id=device,
        device_id_type=pl.DeviceIdType.MESH,
    )
    copy.start()
    return copy


def greet(devices):
    barrier = pltpu.get_barrier_semaphore()
    for device in devices:
        pl.semaphore_signal(
            barrier, inc=1, device_id=device, device_id_type=pl.DeviceIdType.MESH
        )
    pl.semaphore_wait(barrier, len(devices))


def dot(first, second, first_axis=1, second_axis=0):
    return lax.dot_general(
        first,
        second,
        (((first_axis,), (second_axis,)), ((), ())),
        preferred_element_type=jnp.float32,
    )


def parts(value):
    upper = value.astype(jnp.bfloat16)
    lower = (value - upper.astype(jnp.float32)).astype(jnp.bfloat16)
    return upper, lower


def multiply(first, second, first_axis=1, second_axis=0):
    half = first[0].shape[1 - first_axis] // 2
    halves = []
    for rows in (slice(0, half), slice(half, 2 * half)):
        upper, lower = [
            part[rows] if first_axis else part[:, rows] for part in first
        ]
        halves.append(
            dot(upper, second[0], first_axis, second_axis)
            + (
                dot(upper, second[1], first_axis, second_axis)
                + dot(lower, second[0], first_axis, second_axis)
            )
        )
    return jnp.concatenate(halves, axis=0)


def total(value):
    return jnp.sum(jnp.sum(value, axis=0, keepdims=True), axis=1, keepdims=True)


def arrival(target, sem):
    pltpu.make_async_copy(target, target, sem).wait()


def step_kernel(
    reps,
    owns,
    unit,
    sizes,
    owner_in,
    gradients_ref,
    left_ref,
    right_ref,
    left_root_ref,
    right_root_ref,
    first_ref,
    second_ref,
    master_ref,
    new_left_ref,
    new_right_ref,
    new_first_ref,
    new_second_ref,
    weights_ref,
    owner_ref,
    staged,
    raw,
    partial,
    arrived,
    piece_sum,
    summed,
    other,
    roots,
    left_in,
    right_in,
    first_in,
    second_in,
    master_in,
    fifth,
    upper,
    lower,
    current,
    kept,
    outgoing,
    gathered,
    load_sem,
    mine_sem,
    raw_send,
    raw_recv,
    own_send,
    own_recv,
    sum_send,
    sum_recv,
    other_send,
    other_recv,
    row_send,
    row_recv,
):
    rep = lax.axis_index("rep")
    own = lax.axis_index("own")
    block_count = owner_ref.shape[0]
    capacity = new_left_ref.shape[0]
    block_size = new_left_ref.shape[-1]
    row_count = weights_ref.shape[1]
    units = row_count // unit
    groups = reps // capacity
    high = lax.div(rep, capacity)
    low = lax.rem(rep, capacity)
    sides = range(2)
    chunks = len(sizes)
    firsts = [sum(sizes[:chunk]) for chunk in range(chunks)]

    def rep_device(target):
        return (target, own)

    def own_device(target):
        return (rep, target)

    pair_rows = pl.ds(
        pl.multiple_of(high * capacity * row_count, capacity * row_count), capacity * row_count
    )
    mine = pltpu.make_async_copy(gradients_ref, staged, mine_sem.at[0])
    mine.start()
    owners = pltpu.make_async_copy(owner_in, owner_ref, mine_sem.at[1])
    owners.start()
    greet(
        [own_device(lax.rem(own + step, owns)) for step in range(1, owns)]
        + [rep_device(lax.rem(rep + step, reps)) for step in range(1, reps)]
    )
    mine.wait()
    def flipped_bits(step):
        target = jnp.int32(0)
        for bit in range((reps - 1).bit_length()):
            digit = lax.rem(lax.div(rep, 1 << bit), 2)
            target = target + (1 << bit) * lax.rem(digit + (step >> bit & 1), 2)
        return target

    peers = [
        (step, flipped_bits(step))
        for step in sorted(range(1, reps), key=lambda step: -(step >> 1).bit_count())
    ]

    def far(turn):
        down = owns - 1 - turn
        down = down - jnp.where(down <= own, 1, 0)
        up = turn + jnp.where(turn >= own, 1, 0)
        return jnp.where(own < owns // 2, down, up)

    for chunk in range(chunks):
        for step, target in peers:
            send(
                staged.at[:, pl.ds(target * units + firsts[chunk], sizes[chunk])],
                raw[chunk].at[step],
                raw_send.at[chunk],
                raw_recv.at[chunk],
                rep_device(target),
            )
    loads = []
    for place, (source_ref, target_ref) in enumerate(
        (
            (left_root_ref.at[low], roots.at[0]),
            (right_root_ref.at[low], roots.at[1]),
            (left_ref, left_in),
            (right_ref, right_in),
            (first_ref, first_in),
            (second_ref, second_in),
            (master_ref.at[low, pair_rows, :], master_in),
        )
    ):
        loads.append(pltpu.make_async_copy(source_ref, target_ref, load_sem.at[place]))
        loads[-1].start()
    owners.wait()
    slots = [slot_of(owner_ref, block, capacity) for block in range(block_count)]

    def source(slot):
        found = jnp.int32(0)
        for block in range(block_count):
            found = found + jnp.where(slots[block] == slot, block, 0)
        return found

    loads[0].wait()
    loads[1].wait()
    squares = [parts(dot(roots[side], roots[side])) for side in sides]
    fourths = [parts(multiply(squares[side], squares[side])) for side in sides]
    for side in sides:
        fifth[side] = dot(roots[side], fourths[side][0]) + dot(roots[side], fourths[side][1])

    for chunk in range(chunks):
        arrival(raw[chunk].at[1:reps], raw_recv.at[chunk])
        for turn in range(owns):
            target = far(turn) if turn < owns - 1 else own
            step = lax.rem(target - own + owns, owns) if turn < owns - 1 else 0
            for place in range(capacity):
                block = source(target * capacity + place)
                value = staged[
                    block, pl.ds(rep * units + firsts[chunk], sizes[chunk])
                ].astype(jnp.float32)
                for peer in range(1, reps):
                    value = value + raw[chunk][peer, block].astype(jnp.float32)
                partial[chunk][step, place] = value.reshape(sizes[chunk] * unit, block_size)
            if turn < owns - 1:
                send(
                    partial[chunk].at[step],
                    arrived[chunk].at[step],
                    own_send.at[chunk],
                    own_recv.at[chunk],
                    own_device(target),
                )

    for chunk in range(chunks):
        arrival(arrived[chunk].at[1:owns], own_recv.at[chunk])
        value = partial[chunk][0]
        for step in range(1, owns):
            value = value + arrived[chunk][step]
        piece_sum[chunk][...] = value
        start = pl.multiple_of(rep * row_count + firsts[chunk] * unit, unit)
        rows = pl.ds(start, sizes[chunk] * unit)
        for step, target in peers:
            send(
                piece_sum[chunk].at[lax.rem(target, capacity)],
                summed.at[rows, :],
                sum_send.at[0],
                sum_recv.at[0],
                rep_device(target),
            )
        summed[rows, :] = piece_sum[chunk][low]
    for copy in loads[2:]:
        copy.wait()
    arrival(summed.at[0 : block_size - row_count], sum_recv.at[0])
    others = [
        send(
            summed,
            other.at[step],
            other_send.at[step],
            other_recv.at[step],
            rep_device(high * capacity + lax.rem(low + step, capacity)),
        )
        for step in range(1, capacity)
    ]

    scale = (1.0 - stat_decay) / block_size

    def occupied(place):
        count = jnp.int32(0)
        for block in range(block_count):
            count = count + jnp.where(slots[block] == own * capacity + place, 1, 0)
        return count > 0

    def moments(place, gradient, held):
        first_new = first_decay * first_in[place] + (1.0 - first_decay) * gradient
        second_new = (
            second_decay * second_in[place] + (1.0 - second_decay) * gradient * gradient
        )
        new_first_ref[place] = jnp.where(held, first_new, first_in[place])
        new_second_ref[place] = jnp.where(held, second_new, second_in[place])
        return first_new, second_new

    def statistics(place, gradient, held):
        split, flipped = parts(gradient), parts(gradient.T)
        left = stat_decay * left_in[place] + scale * multiply(split, flipped)
        right = stat_decay * right_in[place] + scale * multiply(flipped, split)
        new_left_ref[place] = jnp.where(held, left, left_in[place])
        new_right_ref[place] = jnp.where(held, right, right_in[place])
        return left, right

    held = occupied(low)
    gradient = summed[...]
    for side, value in enumerate(statistics(low, gradient, held)):
        upper[side], lower[side] = parts(value)

    def statistic(side):
        return upper[side], lower[side]

    for side in sides:
        current[side] = (
            5.0 * roots[side].astype(jnp.float32)
            - multiply(parts(fifth[side]), statistic(side))
        ) / 4.0
    first_new, second_new = moments(low, gradient, held)
    adam_step = first_new / (jnp.sqrt(second_new) + 1e-08)
    adam_norm = jnp.sqrt(total(adam_step * adam_step))

    def newton(iteration, carry):
        split = [parts(current[side]) for side in sides]
        squares = [parts(multiply(split[side], split[side])) for side in sides]
        rests = [parts(multiply(squares[side], statistic(side))) for side in sides]
        cubes = [parts(multiply(split[side], squares[side])) for side in sides]
        for side in sides:
            current[side] = (5.0 * current[side] - multiply(cubes[side], rests[side])) / 4.0
        return carry

    for iteration in range(1, NEWTON):
        newton(iteration, 0)

    halfway = multiply(parts(current[0]), parts(summed[...]))
    precond = multiply(parts(halfway), parts(current[1]))
    graft = adam_norm / (jnp.sqrt(total(precond * precond)) + 1e-06)
    kept[...] = precond
    weight = (master_in[...] - learning_rate * graft * kept[pair_rows, :]).astype(jnp.bfloat16)
    for member in range(capacity):
        outgoing[member] = weight[member * row_count : (member + 1) * row_count]
    for turn in range(owns):
        target = far(turn) if turn < owns - 1 else own
        step = lax.rem(target - own + owns, owns) if turn < owns - 1 else 0
        for shift in range(capacity):
            if turn < owns - 1 or shift:
                member = lax.rem(low + shift, capacity)
                send(
                    outgoing.at[member],
                    gathered.at[step * capacity + low],
                    row_send.at[0],
                    row_recv.at[0],
                    (high * capacity + member, target),
                )
    gathered[low] = outgoing[low]

    for step in range(1, capacity):
        others[step - 1].wait_recv()
        place = lax.rem(low + capacity - step, capacity)
        gradient = other[step]
        held = occupied(place)
        statistics(place, gradient, held)
        moments(place, gradient, held)
    for chunk in range(chunks):
        arrival(raw[chunk].at[1:reps], raw_send.at[chunk])
        arrival(arrived[chunk].at[1:owns], own_send.at[chunk])
    arrival(summed.at[0 : block_size - row_count], sum_send.at[0])
    for copy in others:
        copy.wait_send()
    arrival(gathered.at[1 : owns * capacity], row_send.at[0])
    arrival(gathered.at[1 : owns * capacity], row_recv.at[0])
    for block in range(block_count):
        step = lax.rem(own + owns - owner_ref[block], owns)
        place = jnp.minimum(slots[block] - owner_ref[block] * capacity, capacity - 1)
        weights_ref[block] = gathered[step * capacity + place]


def write(*refs):
    count = (len(refs) - 1) // 2
    stores = []
    for index in range(count):
        source_ref, target_ref = refs[index], refs[count + index]
        stores.append(pltpu.make_async_copy(source_ref, target_ref, refs[-1].at[index]))
        stores[-1].start()
    for store in stores:
        store.wait()


def local(
    reps,
    owns,
    gradients,
    owner_index,
    left_stats,
    right_stats,
    left_roots,
    right_roots,
    first_moment,
    second_moment,
    master,
):
    capacity = left_stats.shape[0]
    block_size = left_stats.shape[-1]
    block_count = owner_index.shape[0]
    row_count = block_size // reps
    unit = 8
    sizes = (1, 1, 1, 1) if row_count == 4 * unit else (row_count // unit,)
    chunks = len(sizes)
    vmem = pl.BlockSpec(memory_space=pltpu.VMEM)
    hbm = pl.BlockSpec(memory_space=pltpu.HBM)
    dma = pltpu.SemaphoreType.DMA
    square = (block_size, block_size)
    pieces = [(capacity, size * unit, block_size) for size in sizes]
    whole = (capacity, *square)
    double = (2, *square)
    shapes = [(whole, jnp.float32)] * 4 + [((block_count, row_count, block_size), jnp.bfloat16)]

    results = pl.pallas_call(
        functools.partial(step_kernel, reps, owns, unit, sizes),
        out_shape=[pltpu.VMEM(*leaf) for leaf in shapes],
        in_specs=[hbm] * 9,
        out_specs=[vmem] * 5,
        scratch_shapes=[
            pltpu.SMEM((block_count,), jnp.int32),
            pltpu.VMEM((block_count, block_size // unit, unit, block_size), jnp.bfloat16),
            tuple(
                pltpu.VMEM((reps, block_count, size, unit, block_size), jnp.bfloat16)
                for size in sizes
            ),
            tuple(pltpu.VMEM((owns, *piece), jnp.float32) for piece in pieces),
            tuple(pltpu.VMEM((owns, *piece), jnp.float32) for piece in pieces),
            tuple(pltpu.VMEM(piece, jnp.float32) for piece in pieces),
            pltpu.VMEM(square, jnp.float32),
            pltpu.VMEM(whole, jnp.float32),
            pltpu.VMEM(double, jnp.bfloat16),
            pltpu.VMEM(whole, jnp.float32),
            pltpu.VMEM(whole, jnp.float32),
            pltpu.VMEM(whole, jnp.float32),
            pltpu.VMEM(whole, jnp.float32),
            pltpu.VMEM((capacity * row_count, block_size), jnp.float32),
            pltpu.VMEM(double, jnp.float32),
            pltpu.VMEM(double, jnp.bfloat16),
            pltpu.VMEM(double, jnp.bfloat16),
            pltpu.VMEM(double, jnp.float32),
            pltpu.VMEM(square, jnp.float32),
            pltpu.VMEM((capacity, row_count, block_size), jnp.bfloat16),
            pltpu.VMEM((owns * capacity, row_count, block_size), jnp.bfloat16),
            dma((7,)),
            dma((2,)),
            dma((chunks,)),
            dma((chunks,)),
            dma((chunks,)),
            dma((chunks,)),
            dma((1,)),
            dma((1,)),
            dma((capacity,)),
            dma((capacity,)),
            dma((1,)),
            dma((1,)),
        ],
        compiler_params=pltpu.CompilerParams(
            collective_id=0, has_side_effects=True, vmem_limit_bytes=VMEM_UNITS * 2**18
        ),
        name="step",
    )(
        owner_index,
        gradients.reshape(block_count, block_size // unit, unit, block_size),
        left_stats,
        right_stats,
        left_roots,
        right_roots,
        first_moment,
        second_moment,
        master,
    )
    return tuple(
        pl.pallas_call(
            write,
            out_shape=[jax.ShapeDtypeStruct(*leaf) for leaf in shapes],
            in_specs=[vmem] * 5,
            out_specs=[hbm] * 5,
            scratch_shapes=[dma((5,))],
            compiler_params=pltpu.CompilerParams(vmem_limit_bytes=VMEM_UNITS * 2**18),
            name="write",
        )(*[pltpu.with_memory_space_constraint(leaf, pltpu.VMEM) for leaf in results])
    )


def solution(mesh):
    return jax.shard_map(
        functools.partial(local, mesh.shape["rep"], mesh.shape["own"]),
        mesh=mesh,
        in_specs=(
            P("rep", "own", None, None, None),
            P(),
            P("own", None, None),
            P("own", None, None),
            P("own", None, None),
            P("own", None, None),
            P("own", None, None),
            P("own", None, None),
            P("own", None, None),
        ),
        out_specs=(
            P("own", None, None),
            P("own", None, None),
            P("own", None, None),
            P("own", None, None),
            P(None, "rep", None),
        ),
        check_vma=False,
    )
```

```python
import functools

import jax
import jax.numpy as jnp
from jax import lax
from jax.experimental import pallas as pl
from jax.experimental.pallas import tpu as pltpu
from jax.sharding import PartitionSpec as P

NEWTON = 4
VMEM_UNITS = 246


stat_decay = 0.95
first_decay = 0.9
second_decay = 0.99
learning_rate = 0.5


def slot_of(owner_ref, block, capacity):
    rank = jnp.int32(0)
    for earlier in range(block):
        rank = rank + jnp.where(owner_ref[earlier] == owner_ref[block], 1, 0)
    return owner_ref[block] * capacity + rank


def send(source, target, send_sem, recv_sem, device):
    copy = pltpu.make_async_remote_copy(
        src_ref=source,
        dst_ref=target,
        send_sem=send_sem,
        recv_sem=recv_sem,
        device_id=device,
        device_id_type=pl.DeviceIdType.MESH,
    )
    copy.start()
    return copy


def signal(semaphore, device):
    pl.semaphore_signal(
        semaphore, inc=1, device_id=device, device_id_type=pl.DeviceIdType.MESH
    )


def dot(first, second, first_axis=1, second_axis=0):
    return lax.dot_general(
        first,
        second,
        (((first_axis,), (second_axis,)), ((), ())),
        preferred_element_type=jnp.float32,
    )


def parts(value):
    upper = value.astype(jnp.bfloat16)
    lower = (value - upper.astype(jnp.float32)).astype(jnp.bfloat16)
    return upper, lower


def multiply(first, second, first_axis=1, second_axis=0):
    half = first[0].shape[1 - first_axis] // 2
    halves = []
    for rows in (slice(0, half), slice(half, 2 * half)):
        upper, lower = [
            part[rows] if first_axis else part[:, rows] for part in first
        ]
        halves.append(
            dot(upper, second[0], first_axis, second_axis)
            + (
                dot(upper, second[1], first_axis, second_axis)
                + dot(lower, second[0], first_axis, second_axis)
            )
        )
    return jnp.concatenate(halves, axis=0)


def total(value):
    return jnp.sum(jnp.sum(value, axis=0, keepdims=True), axis=1, keepdims=True)


def arrival(target, sem):
    pltpu.make_async_copy(target, target, sem).wait()


def step_kernel(
    reps,
    owns,
    unit,
    sizes,
    owner_in,
    gradients_ref,
    left_ref,
    right_ref,
    left_root_ref,
    right_root_ref,
    first_ref,
    second_ref,
    master_ref,
    new_left_ref,
    new_right_ref,
    new_first_ref,
    new_second_ref,
    weights_ref,
    owner_ref,
    staged,
    raw,
    partial,
    arrived,
    piece_sum,
    summed,
    other,
    roots,
    left_in,
    right_in,
    first_in,
    second_in,
    master_in,
    fifth,
    upper,
    lower,
    current,
    kept,
    outgoing,
    gathered,
    load_sem,
    mine_sem,
    raw_send,
    raw_recv,
    own_send,
    own_recv,
    sum_send,
    sum_recv,
    other_send,
    other_recv,
    row_send,
    row_recv,
    plane_sem,
    ready_sem,
):
    rep = lax.axis_index("rep")
    own = lax.axis_index("own")
    block_count = owner_ref.shape[0]
    capacity = new_left_ref.shape[0]
    block_size = new_left_ref.shape[-1]
    row_count = weights_ref.shape[1]
    units = row_count // unit
    groups = reps // capacity
    high = lax.div(rep, capacity)
    low = lax.rem(rep, capacity)
    sides = range(2)
    chunks = len(sizes)
    firsts = [sum(sizes[:chunk]) for chunk in range(chunks)]

    def rep_device(target):
        return (target, own)

    def own_device(target):
        return (rep, target)

    pair_rows = pl.ds(
        pl.multiple_of(high * capacity * row_count, capacity * row_count), capacity * row_count
    )
    mine = pltpu.make_async_copy(gradients_ref, staged, mine_sem.at[0])
    mine.start()
    owners = pltpu.make_async_copy(owner_in, owner_ref, mine_sem.at[1])
    owners.start()
    gate, helper = reps - 1, reps - 2
    barrier = pltpu.get_barrier_semaphore()
    for target in range(reps - 1):

        @pl.when(rep != target)
        def _():
            signal(barrier, rep_device(target))

    @pl.when(rep != gate)
    def _():
        pl.semaphore_wait(barrier, reps - 1)

    @pl.when(rep == helper)
    def _():
        signal(plane_sem, rep_device(gate))
        for step in range(1, owns):
            signal(barrier, (gate, lax.rem(own + step, owns)))

    @pl.when(rep == gate)
    def _():
        pl.semaphore_wait(plane_sem, 1)

    mine.wait()
    def flipped_bits(step):
        target = jnp.int32(0)
        for bit in range((reps - 1).bit_length()):
            digit = lax.rem(lax.div(rep, 1 << bit), 2)
            target = target + (1 << bit) * lax.rem(digit + (step >> bit & 1), 2)
        return target

    peers = [
        (step, flipped_bits(step))
        for step in sorted(range(1, reps), key=lambda step: -(step >> 1).bit_count())
    ]

    def far(turn):
        down = owns - 1 - turn
        down = down - jnp.where(down <= own, 1, 0)
        up = turn + jnp.where(turn >= own, 1, 0)
        return jnp.where(own < owns // 2, down, up)

    for chunk in range(chunks):
        for step, target in peers:
            send(
                staged.at[:, pl.ds(target * units + firsts[chunk], sizes[chunk])],
                raw[chunk].at[step],
                raw_send.at[chunk],
                raw_recv.at[chunk],
                rep_device(target),
            )
    loads = []
    for place, (source_ref, target_ref) in enumerate(
        (
            (left_root_ref.at[low], roots.at[0]),
            (right_root_ref.at[low], roots.at[1]),
            (left_ref, left_in),
            (right_ref, right_in),
            (first_ref, first_in),
            (second_ref, second_in),
            (master_ref.at[low, pair_rows, :], master_in),
        )
    ):
        loads.append(pltpu.make_async_copy(source_ref, target_ref, load_sem.at[place]))
        loads[-1].start()
    @pl.when(rep == gate)
    def _():
        pl.semaphore_wait(barrier, owns - 1)
        for target in range(reps - 1):
            signal(ready_sem, rep_device(target))

    owners.wait()
    slots = [slot_of(owner_ref, block, capacity) for block in range(block_count)]

    def source(slot):
        found = jnp.int32(0)
        for block in range(block_count):
            found = found + jnp.where(slots[block] == slot, block, 0)
        return found

    loads[0].wait()
    loads[1].wait()
    squares = [parts(dot(roots[side], roots[side])) for side in sides]
    fourths = [parts(multiply(squares[side], squares[side])) for side in sides]
    for side in sides:
        fifth[side] = dot(roots[side], fourths[side][0]) + dot(roots[side], fourths[side][1])

    for chunk in range(chunks):
        arrival(raw[chunk].at[1:reps], raw_recv.at[chunk])
        if chunk == 0:

            @pl.when(rep != gate)
            def _():
                pl.semaphore_wait(ready_sem, 1)

        for turn in range(owns):
            target = far(turn) if turn < owns - 1 else own
            step = lax.rem(target - own + owns, owns) if turn < owns - 1 else 0
            for place in range(capacity):
                block = source(target * capacity + place)
                value = staged[
                    block, pl.ds(rep * units + firsts[chunk], sizes[chunk])
                ].astype(jnp.float32)
                for peer in range(1, reps):
                    value = value + raw[chunk][peer, block].astype(jnp.float32)
                partial[chunk][step, place] = value.reshape(sizes[chunk] * unit, block_size)
            if turn < owns - 1:
                send(
                    partial[chunk].at[step],
                    arrived[chunk].at[step],
                    own_send.at[chunk],
                    own_recv.at[chunk],
                    own_device(target),
                )

    for chunk in range(chunks):
        arrival(arrived[chunk].at[1:owns], own_recv.at[chunk])
        value = partial[chunk][0]
        for step in range(1, owns):
            value = value + arrived[chunk][step]
        piece_sum[chunk][...] = value
        start = pl.multiple_of(rep * row_count + firsts[chunk] * unit, unit)
        rows = pl.ds(start, sizes[chunk] * unit)
        for step, target in peers:
            send(
                piece_sum[chunk].at[lax.rem(target, capacity)],
                summed.at[rows, :],
                sum_send.at[0],
                sum_recv.at[0],
                rep_device(target),
            )
        summed[rows, :] = piece_sum[chunk][low]
    for copy in loads[2:]:
        copy.wait()
    arrival(summed.at[0 : block_size - row_count], sum_recv.at[0])
    others = [
        send(
            summed,
            other.at[step],
            other_send.at[step],
            other_recv.at[step],
            rep_device(high * capacity + lax.rem(low + step, capacity)),
        )
        for step in range(1, capacity)
    ]

    scale = (1.0 - stat_decay) / block_size

    def occupied(place):
        count = jnp.int32(0)
        for block in range(block_count):
            count = count + jnp.where(slots[block] == own * capacity + place, 1, 0)
        return count > 0

    def moments(place, gradient, held):
        first_new = first_decay * first_in[place] + (1.0 - first_decay) * gradient
        second_new = (
            second_decay * second_in[place] + (1.0 - second_decay) * gradient * gradient
        )
        new_first_ref[place] = jnp.where(held, first_new, first_in[place])
        new_second_ref[place] = jnp.where(held, second_new, second_in[place])
        return first_new, second_new

    def statistics(place, gradient, held):
        split, flipped = parts(gradient), parts(gradient.T)
        left = stat_decay * left_in[place] + scale * multiply(split, flipped)
        right = stat_decay * right_in[place] + scale * multiply(flipped, split)
        new_left_ref[place] = jnp.where(held, left, left_in[place])
        new_right_ref[place] = jnp.where(held, right, right_in[place])
        return left, right

    held = occupied(low)
    gradient = summed[...]
    for side, value in enumerate(statistics(low, gradient, held)):
        upper[side], lower[side] = parts(value)

    def statistic(side):
        return upper[side], lower[side]

    for side in sides:
        current[side] = (
            5.0 * roots[side].astype(jnp.float32)
            - multiply(parts(fifth[side]), statistic(side))
        ) / 4.0
    first_new, second_new = moments(low, gradient, held)
    adam_step = first_new / (jnp.sqrt(second_new) + 1e-08)
    adam_norm = jnp.sqrt(total(adam_step * adam_step))

    def newton(iteration, carry):
        split = [parts(current[side]) for side in sides]
        squares = [parts(multiply(split[side], split[side])) for side in sides]
        rests = [parts(multiply(squares[side], statistic(side))) for side in sides]
        cubes = [parts(multiply(split[side], squares[side])) for side in sides]
        for side in sides:
            current[side] = (5.0 * current[side] - multiply(cubes[side], rests[side])) / 4.0
        return carry

    for iteration in range(1, NEWTON):
        newton(iteration, 0)

    halfway = multiply(parts(current[0]), parts(summed[...]))
    precond = multiply(parts(halfway), parts(current[1]))
    graft = adam_norm / (jnp.sqrt(total(precond * precond)) + 1e-06)
    kept[...] = precond
    weight = (master_in[...] - learning_rate * graft * kept[pair_rows, :]).astype(jnp.bfloat16)
    for member in range(capacity):
        outgoing[member] = weight[member * row_count : (member + 1) * row_count]
    for turn in range(owns):
        target = far(turn) if turn < owns - 1 else own
        step = lax.rem(target - own + owns, owns) if turn < owns - 1 else 0
        for shift in range(capacity):
            if turn < owns - 1 or shift:
                member = lax.rem(low + shift, capacity)
                send(
                    outgoing.at[member],
                    gathered.at[step * capacity + low],
                    row_send.at[0],
                    row_recv.at[0],
                    (high * capacity + member, target),
                )
    gathered[low] = outgoing[low]

    for step in range(1, capacity):
        others[step - 1].wait_recv()
        place = lax.rem(low + capacity - step, capacity)
        gradient = other[step]
        held = occupied(place)
        statistics(place, gradient, held)
        moments(place, gradient, held)
    for chunk in range(chunks):
        arrival(raw[chunk].at[1:reps], raw_send.at[chunk])
        arrival(arrived[chunk].at[1:owns], own_send.at[chunk])
    arrival(summed.at[0 : block_size - row_count], sum_send.at[0])
    for copy in others:
        copy.wait_send()
    arrival(gathered.at[1 : owns * capacity], row_send.at[0])
    arrival(gathered.at[1 : owns * capacity], row_recv.at[0])
    for block in range(block_count):
        step = lax.rem(own + owns - owner_ref[block], owns)
        place = jnp.minimum(slots[block] - owner_ref[block] * capacity, capacity - 1)
        weights_ref[block] = gathered[step * capacity + place]


def write(*refs):
    count = (len(refs) - 1) // 2
    stores = []
    for index in range(count):
        source_ref, target_ref = refs[index], refs[count + index]
        stores.append(pltpu.make_async_copy(source_ref, target_ref, refs[-1].at[index]))
        stores[-1].start()
    for store in stores:
        store.wait()


def local(
    reps,
    owns,
    gradients,
    owner_index,
    left_stats,
    right_stats,
    left_roots,
    right_roots,
    first_moment,
    second_moment,
    master,
):
    capacity = left_stats.shape[0]
    block_size = left_stats.shape[-1]
    block_count = owner_index.shape[0]
    row_count = block_size // reps
    unit = 8
    sizes = (1, 1, 1, 1) if row_count == 4 * unit else (row_count // unit,)
    chunks = len(sizes)
    vmem = pl.BlockSpec(memory_space=pltpu.VMEM)
    hbm = pl.BlockSpec(memory_space=pltpu.HBM)
    dma = pltpu.SemaphoreType.DMA
    square = (block_size, block_size)
    pieces = [(capacity, size * unit, block_size) for size in sizes]
    whole = (capacity, *square)
    double = (2, *square)
    shapes = [(whole, jnp.float32)] * 4 + [((block_count, row_count, block_size), jnp.bfloat16)]

    results = pl.pallas_call(
        functools.partial(step_kernel, reps, owns, unit, sizes),
        out_shape=[pltpu.VMEM(*leaf) for leaf in shapes],
        in_specs=[hbm] * 9,
        out_specs=[vmem] * 5,
        scratch_shapes=[
            pltpu.SMEM((block_count,), jnp.int32),
            pltpu.VMEM((block_count, block_size // unit, unit, block_size), jnp.bfloat16),
            tuple(
                pltpu.VMEM((reps, block_count, size, unit, block_size), jnp.bfloat16)
                for size in sizes
            ),
            tuple(pltpu.VMEM((owns, *piece), jnp.float32) for piece in pieces),
            tuple(pltpu.VMEM((owns, *piece), jnp.float32) for piece in pieces),
            tuple(pltpu.VMEM(piece, jnp.float32) for piece in pieces),
            pltpu.VMEM(square, jnp.float32),
            pltpu.VMEM(whole, jnp.float32),
            pltpu.VMEM(double, jnp.bfloat16),
            pltpu.VMEM(whole, jnp.float32),
            pltpu.VMEM(whole, jnp.float32),
            pltpu.VMEM(whole, jnp.float32),
            pltpu.VMEM(whole, jnp.float32),
            pltpu.VMEM((capacity * row_count, block_size), jnp.float32),
            pltpu.VMEM(double, jnp.float32),
            pltpu.VMEM(double, jnp.bfloat16),
            pltpu.VMEM(double, jnp.bfloat16),
            pltpu.VMEM(double, jnp.float32),
            pltpu.VMEM(square, jnp.float32),
            pltpu.VMEM((capacity, row_count, block_size), jnp.bfloat16),
            pltpu.VMEM((owns * capacity, row_count, block_size), jnp.bfloat16),
            dma((7,)),
            dma((2,)),
            dma((chunks,)),
            dma((chunks,)),
            dma((chunks,)),
            dma((chunks,)),
            dma((1,)),
            dma((1,)),
            dma((capacity,)),
            dma((capacity,)),
            dma((1,)),
            dma((1,)),
            pltpu.SemaphoreType.REGULAR,
            pltpu.SemaphoreType.REGULAR,
        ],
        compiler_params=pltpu.CompilerParams(
            collective_id=0, has_side_effects=True, vmem_limit_bytes=VMEM_UNITS * 2**18
        ),
        name="step",
    )(
        owner_index,
        gradients.reshape(block_count, block_size // unit, unit, block_size),
        left_stats,
        right_stats,
        left_roots,
        right_roots,
        first_moment,
        second_moment,
        master,
    )
    return tuple(
        pl.pallas_call(
            write,
            out_shape=[jax.ShapeDtypeStruct(*leaf) for leaf in shapes],
            in_specs=[vmem] * 5,
            out_specs=[hbm] * 5,
            scratch_shapes=[dma((5,))],
            compiler_params=pltpu.CompilerParams(vmem_limit_bytes=VMEM_UNITS * 2**18),
            name="write",
        )(*[pltpu.with_memory_space_constraint(leaf, pltpu.VMEM) for leaf in results])
    )


def solution(mesh):
    return jax.shard_map(
        functools.partial(local, mesh.shape["rep"], mesh.shape["own"]),
        mesh=mesh,
        in_specs=(
            P("rep", "own", None, None, None),
            P(),
            P("own", None, None),
            P("own", None, None),
            P("own", None, None),
            P("own", None, None),
            P("own", None, None),
            P("own", None, None),
            P("own", None, None),
        ),
        out_specs=(
            P("own", None, None),
            P("own", None, None),
            P("own", None, None),
            P("own", None, None),
            P(None, "rep", None),
        ),
        check_vma=False,
    )
```

```python
import functools

import jax
import jax.numpy as jnp
from jax import lax
from jax.experimental import pallas as pl
from jax.experimental.pallas import tpu as pltpu
from jax.sharding import PartitionSpec as P

NEWTON = 4
VMEM_UNITS = 246


stat_decay = 0.95
first_decay = 0.9
second_decay = 0.99
learning_rate = 0.5


def slot_of(owner_ref, block, capacity):
    rank = jnp.int32(0)
    for earlier in range(block):
        rank = rank + jnp.where(owner_ref[earlier] == owner_ref[block], 1, 0)
    return owner_ref[block] * capacity + rank


def send(source, target, send_sem, recv_sem, device):
    copy = pltpu.make_async_remote_copy(
        src_ref=source,
        dst_ref=target,
        send_sem=send_sem,
        recv_sem=recv_sem,
        device_id=device,
        device_id_type=pl.DeviceIdType.MESH,
    )
    copy.start()
    return copy


def signal(semaphore, device):
    pl.semaphore_signal(
        semaphore, inc=1, device_id=device, device_id_type=pl.DeviceIdType.MESH
    )


def dot(first, second, first_axis=1, second_axis=0):
    return lax.dot_general(
        first,
        second,
        (((first_axis,), (second_axis,)), ((), ())),
        preferred_element_type=jnp.float32,
    )


def parts(value):
    upper = value.astype(jnp.bfloat16)
    lower = (value - upper.astype(jnp.float32)).astype(jnp.bfloat16)
    return upper, lower


def multiply(first, second, first_axis=1, second_axis=0):
    half = first[0].shape[1 - first_axis] // 2
    halves = []
    for rows in (slice(0, half), slice(half, 2 * half)):
        upper, lower = [
            part[rows] if first_axis else part[:, rows] for part in first
        ]
        halves.append(
            dot(upper, second[0], first_axis, second_axis)
            + (
                dot(upper, second[1], first_axis, second_axis)
                + dot(lower, second[0], first_axis, second_axis)
            )
        )
    return jnp.concatenate(halves, axis=0)


def total(value):
    return jnp.sum(jnp.sum(value, axis=0, keepdims=True), axis=1, keepdims=True)


def arrival(target, sem):
    pltpu.make_async_copy(target, target, sem).wait()


def step_kernel(
    reps,
    owns,
    unit,
    pieces,
    owner_in,
    gradients_ref,
    left_ref,
    right_ref,
    left_root_ref,
    right_root_ref,
    first_ref,
    second_ref,
    master_ref,
    new_left_ref,
    new_right_ref,
    new_first_ref,
    new_second_ref,
    weights_ref,
    owner_ref,
    staged,
    raw,
    partial,
    arrived,
    piece_sum,
    summed,
    other,
    roots,
    left_in,
    right_in,
    first_in,
    second_in,
    master_in,
    fifth,
    upper,
    lower,
    current,
    kept,
    outgoing,
    gathered,
    load_sem,
    mine_sem,
    raw_send,
    raw_recv,
    own_send,
    own_recv,
    sum_send,
    sum_recv,
    other_send,
    other_recv,
    row_send,
    row_recv,
    plane_sem,
    ready_sem,
):
    rep = lax.axis_index("rep")
    own = lax.axis_index("own")
    block_count = owner_ref.shape[0]
    capacity = new_left_ref.shape[0]
    block_size = new_left_ref.shape[-1]
    row_count = weights_ref.shape[1]
    units = row_count // unit
    groups = reps // capacity
    high = lax.div(rep, capacity)
    low = lax.rem(rep, capacity)
    sides = range(2)
    chunks = len(pieces)

    def part(chunk, device):
        first, size, column, width = pieces[chunk]
        return pl.ds(device * units + first, size), slice(None), slice(column, column + width)


    def rep_device(target):
        return (target, own)

    def own_device(target):
        return (rep, target)

    pair_rows = pl.ds(
        pl.multiple_of(high * capacity * row_count, capacity * row_count), capacity * row_count
    )
    mine = pltpu.make_async_copy(gradients_ref, staged, mine_sem.at[0])
    mine.start()
    owners = pltpu.make_async_copy(owner_in, owner_ref, mine_sem.at[1])
    owners.start()
    gate, helper = reps - 1, reps - 2
    barrier = pltpu.get_barrier_semaphore()
    for target in range(reps - 1):

        @pl.when(rep != target)
        def _():
            signal(barrier, rep_device(target))

    @pl.when(rep != gate)
    def _():
        pl.semaphore_wait(barrier, reps - 1)

    @pl.when(rep == helper)
    def _():
        signal(plane_sem, rep_device(gate))
        for step in range(1, owns):
            signal(barrier, (gate, lax.rem(own + step, owns)))

    @pl.when(rep == gate)
    def _():
        pl.semaphore_wait(plane_sem, 1)

    mine.wait()
    def flipped_bits(step):
        target = jnp.int32(0)
        for bit in range((reps - 1).bit_length()):
            digit = lax.rem(lax.div(rep, 1 << bit), 2)
            target = target + (1 << bit) * lax.rem(digit + (step >> bit & 1), 2)
        return target

    peers = [
        (step, flipped_bits(step))
        for step in sorted(
            range(1, reps), key=lambda step: (-(step >> 1).bit_count(), step >> 1, -step)
        )
    ]

    def far(turn):
        down = owns - 1 - turn
        down = down - jnp.where(down <= own, 1, 0)
        up = turn + jnp.where(turn >= own, 1, 0)
        return jnp.where(own < owns // 2, down, up)

    for chunk in range(chunks):
        for step, target in peers:
            send(
                staged.at[:, *part(chunk, target)],
                raw[chunk].at[step],
                raw_send.at[chunk],
                raw_recv.at[chunk],
                rep_device(target),
            )
    loads = []
    for place, (source_ref, target_ref) in enumerate(
        (
            (left_root_ref.at[low], roots.at[0]),
            (right_root_ref.at[low], roots.at[1]),
            (left_ref, left_in),
            (right_ref, right_in),
            (first_ref, first_in),
            (second_ref, second_in),
            (master_ref.at[low, pair_rows, :], master_in),
        )
    ):
        loads.append(pltpu.make_async_copy(source_ref, target_ref, load_sem.at[place]))
        loads[-1].start()
    @pl.when(rep == gate)
    def _():
        pl.semaphore_wait(barrier, owns - 1)
        for target in range(reps - 1):
            signal(ready_sem, rep_device(target))

    owners.wait()
    slots = [slot_of(owner_ref, block, capacity) for block in range(block_count)]

    def source(slot):
        found = jnp.int32(0)
        for block in range(block_count):
            found = found + jnp.where(slots[block] == slot, block, 0)
        return found

    loads[0].wait()
    loads[1].wait()
    squares = [parts(dot(roots[side], roots[side])) for side in sides]
    fourths = [parts(multiply(squares[side], squares[side])) for side in sides]
    for side in sides:
        fifth[side] = dot(roots[side], fourths[side][0]) + dot(roots[side], fourths[side][1])

    for chunk in range(chunks):
        arrival(raw[chunk].at[1:reps], raw_recv.at[chunk])
        if chunk == 0:

            @pl.when(rep != gate)
            def _():
                pl.semaphore_wait(ready_sem, 1)

        for turn in range(owns):
            target = far(turn) if turn < owns - 1 else own
            step = lax.rem(target - own + owns, owns) if turn < owns - 1 else 0
            for place in range(capacity):
                block = source(target * capacity + place)
                value = staged[block, *part(chunk, rep)].astype(jnp.float32)
                for peer in range(1, reps):
                    value = value + raw[chunk][peer, block].astype(jnp.float32)
                partial[chunk][step, place] = value.reshape(
                    partial[chunk].shape[2:]
                )
            if turn < owns - 1:
                send(
                    partial[chunk].at[step],
                    arrived[chunk].at[step],
                    own_send.at[chunk],
                    own_recv.at[chunk],
                    own_device(target),
                )

    for chunk in range(chunks):
        arrival(arrived[chunk].at[1:owns], own_recv.at[chunk])
        value = partial[chunk][0]
        for step in range(1, owns):
            value = value + arrived[chunk][step]
        piece_sum[chunk][...] = value
        first, size, column, width = pieces[chunk]
        start = pl.multiple_of(rep * row_count + first * unit, unit)
        rows, columns = pl.ds(start, size * unit), slice(column, column + width)
        for step, target in peers:
            send(
                piece_sum[chunk].at[lax.rem(target, capacity)],
                summed.at[rows, columns],
                sum_send.at[0],
                sum_recv.at[0],
                rep_device(target),
            )
        summed[rows, columns] = piece_sum[chunk][low]
    for copy in loads[2:]:
        copy.wait()
    arrival(summed.at[0 : block_size - row_count], sum_recv.at[0])
    others = [
        send(
            summed,
            other.at[step],
            other_send.at[step],
            other_recv.at[step],
            rep_device(high * capacity + lax.rem(low + step, capacity)),
        )
        for step in range(1, capacity)
    ]

    scale = (1.0 - stat_decay) / block_size

    def occupied(place):
        count = jnp.int32(0)
        for block in range(block_count):
            count = count + jnp.where(slots[block] == own * capacity + place, 1, 0)
        return count > 0

    def moments(place, gradient, held):
        first_new = first_decay * first_in[place] + (1.0 - first_decay) * gradient
        second_new = (
            second_decay * second_in[place] + (1.0 - second_decay) * gradient * gradient
        )
        new_first_ref[place] = jnp.where(held, first_new, first_in[place])
        new_second_ref[place] = jnp.where(held, second_new, second_in[place])
        return first_new, second_new

    def statistics(place, gradient, held):
        split, flipped = parts(gradient), parts(gradient.T)
        left = stat_decay * left_in[place] + scale * multiply(split, flipped)
        right = stat_decay * right_in[place] + scale * multiply(flipped, split)
        new_left_ref[place] = jnp.where(held, left, left_in[place])
        new_right_ref[place] = jnp.where(held, right, right_in[place])
        return left, right

    held = occupied(low)
    gradient = summed[...]
    for side, value in enumerate(statistics(low, gradient, held)):
        upper[side], lower[side] = parts(value)

    def statistic(side):
        return upper[side], lower[side]

    for side in sides:
        current[side] = (
            5.0 * roots[side].astype(jnp.float32)
            - multiply(parts(fifth[side]), statistic(side))
        ) / 4.0
    first_new, second_new = moments(low, gradient, held)
    adam_step = first_new / (jnp.sqrt(second_new) + 1e-08)
    adam_norm = jnp.sqrt(total(adam_step * adam_step))

    def newton(iteration, carry):
        split = [parts(current[side]) for side in sides]
        squares = [parts(multiply(split[side], split[side])) for side in sides]
        rests = [parts(multiply(squares[side], statistic(side))) for side in sides]
        cubes = [parts(multiply(split[side], squares[side])) for side in sides]
        for side in sides:
            current[side] = (5.0 * current[side] - multiply(cubes[side], rests[side])) / 4.0
        return carry

    for iteration in range(1, NEWTON):
        newton(iteration, 0)

    halfway = multiply(parts(current[0]), parts(summed[...]))
    precond = multiply(parts(halfway), parts(current[1]))
    graft = adam_norm / (jnp.sqrt(total(precond * precond)) + 1e-06)
    kept[...] = precond
    weight = (master_in[...] - learning_rate * graft * kept[pair_rows, :]).astype(jnp.bfloat16)
    for member in range(capacity):
        outgoing[member] = weight[member * row_count : (member + 1) * row_count]
    for turn in range(owns):
        target = far(turn) if turn < owns - 1 else own
        step = lax.rem(target - own + owns, owns) if turn < owns - 1 else 0
        for shift in range(capacity):
            if turn < owns - 1 or shift:
                member = lax.rem(low + shift, capacity)
                send(
                    outgoing.at[member],
                    gathered.at[step * capacity + low],
                    row_send.at[0],
                    row_recv.at[0],
                    (high * capacity + member, target),
                )
    gathered[low] = outgoing[low]

    for step in range(1, capacity):
        others[step - 1].wait_recv()
        place = lax.rem(low + capacity - step, capacity)
        gradient = other[step]
        held = occupied(place)
        statistics(place, gradient, held)
        moments(place, gradient, held)
    for chunk in range(chunks):
        arrival(raw[chunk].at[1:reps], raw_send.at[chunk])
        arrival(arrived[chunk].at[1:owns], own_send.at[chunk])
    arrival(summed.at[0 : block_size - row_count], sum_send.at[0])
    for copy in others:
        copy.wait_send()
    arrival(gathered.at[1 : owns * capacity], row_send.at[0])
    arrival(gathered.at[1 : owns * capacity], row_recv.at[0])
    for block in range(block_count):
        step = lax.rem(own + owns - owner_ref[block], owns)
        place = jnp.minimum(slots[block] - owner_ref[block] * capacity, capacity - 1)
        weights_ref[block] = gathered[step * capacity + place]


def write(*refs):
    count = (len(refs) - 1) // 2
    stores = []
    for index in range(count):
        source_ref, target_ref = refs[index], refs[count + index]
        stores.append(pltpu.make_async_copy(source_ref, target_ref, refs[-1].at[index]))
        stores[-1].start()
    for store in stores:
        store.wait()


def local(
    reps,
    owns,
    gradients,
    owner_index,
    left_stats,
    right_stats,
    left_roots,
    right_roots,
    first_moment,
    second_moment,
    master,
):
    capacity = left_stats.shape[0]
    block_size = left_stats.shape[-1]
    block_count = owner_index.shape[0]
    row_count = block_size // reps
    unit = 8
    units = row_count // unit
    half = block_size // 2
    pieces = [(first, 1, column, half) for first in range(units) for column in (0, half)]
    chunks = len(pieces)
    vmem = pl.BlockSpec(memory_space=pltpu.VMEM)
    hbm = pl.BlockSpec(memory_space=pltpu.HBM)
    dma = pltpu.SemaphoreType.DMA
    square = (block_size, block_size)
    piece_shapes = [(capacity, size * unit, width) for _, size, _, width in pieces]
    whole = (capacity, *square)
    double = (2, *square)
    shapes = [(whole, jnp.float32)] * 4 + [((block_count, row_count, block_size), jnp.bfloat16)]

    results = pl.pallas_call(
        functools.partial(step_kernel, reps, owns, unit, pieces),
        out_shape=[pltpu.VMEM(*leaf) for leaf in shapes],
        in_specs=[hbm] * 9,
        out_specs=[vmem] * 5,
        scratch_shapes=[
            pltpu.SMEM((block_count,), jnp.int32),
            pltpu.VMEM((block_count, block_size // unit, unit, block_size), jnp.bfloat16),
            tuple(
                pltpu.VMEM((reps, block_count, size, unit, width), jnp.bfloat16)
                for _, size, _, width in pieces
            ),
            tuple(pltpu.VMEM((owns, *piece), jnp.float32) for piece in piece_shapes),
            tuple(pltpu.VMEM((owns, *piece), jnp.float32) for piece in piece_shapes),
            tuple(pltpu.VMEM(piece, jnp.float32) for piece in piece_shapes),
            pltpu.VMEM(square, jnp.float32),
            pltpu.VMEM(whole, jnp.float32),
            pltpu.VMEM(double, jnp.bfloat16),
            pltpu.VMEM(whole, jnp.float32),
            pltpu.VMEM(whole, jnp.float32),
            pltpu.VMEM(whole, jnp.float32),
            pltpu.VMEM(whole, jnp.float32),
            pltpu.VMEM((capacity * row_count, block_size), jnp.float32),
            pltpu.VMEM(double, jnp.float32),
            pltpu.VMEM(double, jnp.bfloat16),
            pltpu.VMEM(double, jnp.bfloat16),
            pltpu.VMEM(double, jnp.float32),
            pltpu.VMEM(square, jnp.float32),
            pltpu.VMEM((capacity, row_count, block_size), jnp.bfloat16),
            pltpu.VMEM((owns * capacity, row_count, block_size), jnp.bfloat16),
            dma((7,)),
            dma((2,)),
            dma((chunks,)),
            dma((chunks,)),
            dma((chunks,)),
            dma((chunks,)),
            dma((1,)),
            dma((1,)),
            dma((capacity,)),
            dma((capacity,)),
            dma((1,)),
            dma((1,)),
            pltpu.SemaphoreType.REGULAR,
            pltpu.SemaphoreType.REGULAR,
        ],
        compiler_params=pltpu.CompilerParams(
            collective_id=0, has_side_effects=True, vmem_limit_bytes=VMEM_UNITS * 2**18
        ),
        name="step",
    )(
        owner_index,
        gradients.reshape(block_count, block_size // unit, unit, block_size),
        left_stats,
        right_stats,
        left_roots,
        right_roots,
        first_moment,
        second_moment,
        master,
    )
    return tuple(
        pl.pallas_call(
            write,
            out_shape=[jax.ShapeDtypeStruct(*leaf) for leaf in shapes],
            in_specs=[vmem] * 5,
            out_specs=[hbm] * 5,
            scratch_shapes=[dma((5,))],
            compiler_params=pltpu.CompilerParams(vmem_limit_bytes=VMEM_UNITS * 2**18),
            name="write",
        )(*[pltpu.with_memory_space_constraint(leaf, pltpu.VMEM) for leaf in results])
    )


def solution(mesh):
    return jax.shard_map(
        functools.partial(local, mesh.shape["rep"], mesh.shape["own"]),
        mesh=mesh,
        in_specs=(
            P("rep", "own", None, None, None),
            P(),
            P("own", None, None),
            P("own", None, None),
            P("own", None, None),
            P("own", None, None),
            P("own", None, None),
            P("own", None, None),
            P("own", None, None),
        ),
        out_specs=(
            P("own", None, None),
            P("own", None, None),
            P("own", None, None),
            P("own", None, None),
            P(None, "rep", None),
        ),
        check_vma=False,
    )
```

```python
import functools

import jax
import jax.numpy as jnp
from jax import lax
from jax.experimental import pallas as pl
from jax.experimental.pallas import tpu as pltpu
from jax.sharding import PartitionSpec as P

NEWTON = 4
VMEM_UNITS = 246


stat_decay = 0.95
first_decay = 0.9
second_decay = 0.99
learning_rate = 0.5


def slot_of(owner_ref, block, capacity):
    rank = jnp.int32(0)
    for earlier in range(block):
        rank = rank + jnp.where(owner_ref[earlier] == owner_ref[block], 1, 0)
    return owner_ref[block] * capacity + rank


def send(source, target, send_sem, recv_sem, device):
    copy = pltpu.make_async_remote_copy(
        src_ref=source,
        dst_ref=target,
        send_sem=send_sem,
        recv_sem=recv_sem,
        device_id=device,
        device_id_type=pl.DeviceIdType.MESH,
    )
    copy.start()
    return copy


def signal(semaphore, device):
    pl.semaphore_signal(
        semaphore, inc=1, device_id=device, device_id_type=pl.DeviceIdType.MESH
    )


def dot(first, second, first_axis=1, second_axis=0):
    return lax.dot_general(
        first,
        second,
        (((first_axis,), (second_axis,)), ((), ())),
        preferred_element_type=jnp.float32,
    )


def parts(value):
    upper = value.astype(jnp.bfloat16)
    lower = (value - upper.astype(jnp.float32)).astype(jnp.bfloat16)
    return upper, lower


def multiply(first, second, first_axis=1, second_axis=0):
    half = first[0].shape[1 - first_axis] // 2
    halves = []
    for rows in (slice(0, half), slice(half, 2 * half)):
        upper, lower = [
            part[rows] if first_axis else part[:, rows] for part in first
        ]
        halves.append(
            dot(upper, second[0], first_axis, second_axis)
            + (
                dot(upper, second[1], first_axis, second_axis)
                + dot(lower, second[0], first_axis, second_axis)
            )
        )
    return jnp.concatenate(halves, axis=0)


def total(value):
    return jnp.sum(jnp.sum(value, axis=0, keepdims=True), axis=1, keepdims=True)


def arrival(target, sem):
    pltpu.make_async_copy(target, target, sem).wait()


def step_kernel(
    reps,
    owns,
    unit,
    pieces,
    owner_in,
    gradients_ref,
    left_ref,
    right_ref,
    left_root_ref,
    right_root_ref,
    first_ref,
    second_ref,
    master_ref,
    new_left_ref,
    new_right_ref,
    new_first_ref,
    new_second_ref,
    weights_ref,
    owner_ref,
    staged,
    raw,
    partial,
    arrived,
    piece_sum,
    summed,
    other,
    roots,
    left_in,
    right_in,
    first_in,
    second_in,
    master_in,
    fifth,
    upper,
    lower,
    current,
    kept,
    outgoing,
    gathered,
    load_sem,
    mine_sem,
    raw_send,
    raw_recv,
    own_send,
    own_recv,
    sum_send,
    sum_recv,
    other_send,
    other_recv,
    row_send,
    row_recv,
    plane_sem,
    ready_sem,
):
    rep = lax.axis_index("rep")
    own = lax.axis_index("own")
    block_count = owner_ref.shape[0]
    capacity = new_left_ref.shape[0]
    block_size = new_left_ref.shape[-1]
    row_count = weights_ref.shape[1]
    units = row_count // unit
    groups = reps // capacity
    high = lax.div(rep, capacity)
    low = lax.rem(rep, capacity)
    sides = range(2)
    chunks = len(pieces)

    def part(chunk, device):
        first, size, column, width = pieces[chunk]
        return pl.ds(device * units + first, size), slice(None), slice(column, column + width)


    def rep_device(target):
        return (target, own)

    def own_device(target):
        return (rep, target)

    pair_rows = pl.ds(
        pl.multiple_of(high * capacity * row_count, capacity * row_count), capacity * row_count
    )
    mine = pltpu.make_async_copy(gradients_ref, staged, mine_sem.at[0])
    mine.start()
    owners = pltpu.make_async_copy(owner_in, owner_ref, mine_sem.at[1])
    owners.start()
    gate, helper = reps - 1, reps - 2
    barrier = pltpu.get_barrier_semaphore()
    for target in range(reps - 1):

        @pl.when(rep != target)
        def _():
            signal(barrier, rep_device(target))

    @pl.when(rep != gate)
    def _():
        pl.semaphore_wait(barrier, reps - 1)

    @pl.when(rep == helper)
    def _():
        signal(plane_sem, rep_device(gate))
        for step in range(1, owns):
            signal(barrier, (gate, lax.rem(own + step, owns)))

    @pl.when(rep == gate)
    def _():
        pl.semaphore_wait(plane_sem, 1)

    mine.wait()
    def flipped_bits(step):
        target = jnp.int32(0)
        for bit in range((reps - 1).bit_length()):
            digit = lax.rem(lax.div(rep, 1 << bit), 2)
            target = target + (1 << bit) * lax.rem(digit + (step >> bit & 1), 2)
        return target

    peers = [
        (step, flipped_bits(step))
        for step in sorted(
            range(1, reps), key=lambda step: (-(step >> 1).bit_count(), -step)
        )
    ]

    def far(turn):
        down = owns - 1 - turn
        down = down - jnp.where(down <= own, 1, 0)
        up = turn + jnp.where(turn >= own, 1, 0)
        return jnp.where(own < owns // 2, down, up)

    for chunk in range(chunks):
        for step, target in peers:
            send(
                staged.at[:, *part(chunk, target)],
                raw[chunk].at[step],
                raw_send.at[chunk],
                raw_recv.at[chunk],
                rep_device(target),
            )
    loads = []
    for place, (source_ref, target_ref) in enumerate(
        (
            (left_root_ref.at[low], roots.at[0]),
            (right_root_ref.at[low], roots.at[1]),
            (left_ref, left_in),
            (right_ref, right_in),
            (first_ref, first_in),
            (second_ref, second_in),
            (master_ref.at[low, pair_rows, :], master_in),
        )
    ):
        loads.append(pltpu.make_async_copy(source_ref, target_ref, load_sem.at[place]))
        loads[-1].start()
    @pl.when(rep == gate)
    def _():
        pl.semaphore_wait(barrier, owns - 1)
        for target in range(reps - 1):
            signal(ready_sem, rep_device(target))

    owners.wait()
    slots = [slot_of(owner_ref, block, capacity) for block in range(block_count)]

    def source(slot):
        found = jnp.int32(0)
        for block in range(block_count):
            found = found + jnp.where(slots[block] == slot, block, 0)
        return found

    loads[0].wait()
    loads[1].wait()
    squares = [parts(dot(roots[side], roots[side])) for side in sides]
    fourths = [parts(multiply(squares[side], squares[side])) for side in sides]
    for side in sides:
        fifth[side] = dot(roots[side], fourths[side][0]) + dot(roots[side], fourths[side][1])

    for chunk in range(chunks):
        arrival(raw[chunk].at[1:reps], raw_recv.at[chunk])
        if chunk == 0:

            @pl.when(rep != gate)
            def _():
                pl.semaphore_wait(ready_sem, 1)

        for turn in range(owns):
            target = far(turn) if turn < owns - 1 else own
            step = lax.rem(target - own + owns, owns) if turn < owns - 1 else 0
            for place in range(capacity):
                block = source(target * capacity + place)
                value = staged[block, *part(chunk, rep)].astype(jnp.float32)
                for peer in range(1, reps):
                    value = value + raw[chunk][peer, block].astype(jnp.float32)
                partial[chunk][step, place] = value.reshape(
                    partial[chunk].shape[2:]
                )
            if turn < owns - 1:
                send(
                    partial[chunk].at[step],
                    arrived[chunk].at[step],
                    own_send.at[chunk],
                    own_recv.at[chunk],
                    own_device(target),
                )

    for chunk in range(chunks):
        arrival(arrived[chunk].at[1:owns], own_recv.at[chunk])
        value = partial[chunk][0]
        for step in range(1, owns):
            value = value + arrived[chunk][step]
        piece_sum[chunk][...] = value
        first, size, column, width = pieces[chunk]
        start = pl.multiple_of(rep * row_count + first * unit, unit)
        rows, columns = pl.ds(start, size * unit), slice(column, column + width)
        for step, target in peers:
            send(
                piece_sum[chunk].at[lax.rem(target, capacity)],
                summed.at[rows, columns],
                sum_send.at[0],
                sum_recv.at[0],
                rep_device(target),
            )
        summed[rows, columns] = piece_sum[chunk][low]
    for copy in loads[2:]:
        copy.wait()
    arrival(summed.at[0 : block_size - row_count], sum_recv.at[0])
    others = [
        send(
            summed,
            other.at[step],
            other_send.at[step],
            other_recv.at[step],
            rep_device(high * capacity + lax.rem(low + step, capacity)),
        )
        for step in range(1, capacity)
    ]

    scale = (1.0 - stat_decay) / block_size

    def occupied(place):
        count = jnp.int32(0)
        for block in range(block_count):
            count = count + jnp.where(slots[block] == own * capacity + place, 1, 0)
        return count > 0

    def moments(place, gradient, held):
        first_new = first_decay * first_in[place] + (1.0 - first_decay) * gradient
        second_new = (
            second_decay * second_in[place] + (1.0 - second_decay) * gradient * gradient
        )
        new_first_ref[place] = jnp.where(held, first_new, first_in[place])
        new_second_ref[place] = jnp.where(held, second_new, second_in[place])
        return first_new, second_new

    def statistics(place, gradient, held):
        split, flipped = parts(gradient), parts(gradient.T)
        left = stat_decay * left_in[place] + scale * multiply(split, flipped)
        right = stat_decay * right_in[place] + scale * multiply(flipped, split)
        new_left_ref[place] = jnp.where(held, left, left_in[place])
        new_right_ref[place] = jnp.where(held, right, right_in[place])
        return left, right

    held = occupied(low)
    gradient = summed[...]
    for side, value in enumerate(statistics(low, gradient, held)):
        upper[side], lower[side] = parts(value)

    def statistic(side):
        return upper[side], lower[side]

    for side in sides:
        current[side] = (
            5.0 * roots[side].astype(jnp.float32)
            - multiply(parts(fifth[side]), statistic(side))
        ) / 4.0
    first_new, second_new = moments(low, gradient, held)
    adam_step = first_new / (jnp.sqrt(second_new) + 1e-08)
    adam_norm = jnp.sqrt(total(adam_step * adam_step))

    def newton(iteration, carry):
        split = [parts(current[side]) for side in sides]
        squares = [parts(multiply(split[side], split[side])) for side in sides]
        rests = [parts(multiply(squares[side], statistic(side))) for side in sides]
        cubes = [parts(multiply(split[side], squares[side])) for side in sides]
        for side in sides:
            current[side] = 1.25 * current[side] - 0.25 * multiply(cubes[side], rests[side])
        return carry

    for iteration in range(1, NEWTON):
        newton(iteration, 0)

    halfway = multiply(parts(current[0]), parts(summed[...]))
    precond = multiply(parts(halfway), parts(current[1]))
    graft = adam_norm / (jnp.sqrt(total(precond * precond)) + 1e-06)
    kept[...] = precond
    weight = (master_in[...] - learning_rate * graft * kept[pair_rows, :]).astype(jnp.bfloat16)
    for member in range(capacity):
        outgoing[member] = weight[member * row_count : (member + 1) * row_count]
    for turn in range(owns):
        target = far(turn) if turn < owns - 1 else own
        step = lax.rem(target - own + owns, owns) if turn < owns - 1 else 0
        for shift in range(capacity):
            if turn < owns - 1 or shift:
                member = lax.rem(low + shift, capacity)
                send(
                    outgoing.at[member],
                    gathered.at[step * capacity + low],
                    row_send.at[0],
                    row_recv.at[0],
                    (high * capacity + member, target),
                )
    gathered[low] = outgoing[low]

    for step in range(1, capacity):
        others[step - 1].wait_recv()
        place = lax.rem(low + capacity - step, capacity)
        gradient = other[step]
        held = occupied(place)
        statistics(place, gradient, held)
        moments(place, gradient, held)
    for chunk in range(chunks):
        arrival(raw[chunk].at[1:reps], raw_send.at[chunk])
        arrival(arrived[chunk].at[1:owns], own_send.at[chunk])
    arrival(summed.at[0 : block_size - row_count], sum_send.at[0])
    for copy in others:
        copy.wait_send()
    arrival(gathered.at[1 : owns * capacity], row_send.at[0])
    arrival(gathered.at[1 : owns * capacity], row_recv.at[0])
    for block in range(block_count):
        step = lax.rem(own + owns - owner_ref[block], owns)
        place = jnp.minimum(slots[block] - owner_ref[block] * capacity, capacity - 1)
        weights_ref[block] = gathered[step * capacity + place]


def write(*refs):
    count = (len(refs) - 1) // 2
    stores = []
    for index in range(count):
        source_ref, target_ref = refs[index], refs[count + index]
        stores.append(pltpu.make_async_copy(source_ref, target_ref, refs[-1].at[index]))
        stores[-1].start()
    for store in stores:
        store.wait()


def local(
    reps,
    owns,
    gradients,
    owner_index,
    left_stats,
    right_stats,
    left_roots,
    right_roots,
    first_moment,
    second_moment,
    master,
):
    capacity = left_stats.shape[0]
    block_size = left_stats.shape[-1]
    block_count = owner_index.shape[0]
    row_count = block_size // reps
    unit = 8
    units = row_count // unit
    half = block_size // 2
    pieces = [(first, 1, column, half) for first in range(units) for column in (0, half)]
    chunks = len(pieces)
    vmem = pl.BlockSpec(memory_space=pltpu.VMEM)
    hbm = pl.BlockSpec(memory_space=pltpu.HBM)
    dma = pltpu.SemaphoreType.DMA
    square = (block_size, block_size)
    piece_shapes = [(capacity, size * unit, width) for _, size, _, width in pieces]
    whole = (capacity, *square)
    double = (2, *square)
    shapes = [(whole, jnp.float32)] * 4 + [((block_count, row_count, block_size), jnp.bfloat16)]

    results = pl.pallas_call(
        functools.partial(step_kernel, reps, owns, unit, pieces),
        out_shape=[pltpu.VMEM(*leaf) for leaf in shapes],
        in_specs=[hbm] * 9,
        out_specs=[vmem] * 5,
        scratch_shapes=[
            pltpu.SMEM((block_count,), jnp.int32),
            pltpu.VMEM((block_count, block_size // unit, unit, block_size), jnp.bfloat16),
            tuple(
                pltpu.VMEM((reps, block_count, size, unit, width), jnp.bfloat16)
                for _, size, _, width in pieces
            ),
            tuple(pltpu.VMEM((owns, *piece), jnp.float32) for piece in piece_shapes),
            tuple(pltpu.VMEM((owns, *piece), jnp.float32) for piece in piece_shapes),
            tuple(pltpu.VMEM(piece, jnp.float32) for piece in piece_shapes),
            pltpu.VMEM(square, jnp.float32),
            pltpu.VMEM(whole, jnp.float32),
            pltpu.VMEM(double, jnp.bfloat16),
            pltpu.VMEM(whole, jnp.float32),
            pltpu.VMEM(whole, jnp.float32),
            pltpu.VMEM(whole, jnp.float32),
            pltpu.VMEM(whole, jnp.float32),
            pltpu.VMEM((capacity * row_count, block_size), jnp.float32),
            pltpu.VMEM(double, jnp.float32),
            pltpu.VMEM(double, jnp.bfloat16),
            pltpu.VMEM(double, jnp.bfloat16),
            pltpu.VMEM(double, jnp.float32),
            pltpu.VMEM(square, jnp.float32),
            pltpu.VMEM((capacity, row_count, block_size), jnp.bfloat16),
            pltpu.VMEM((owns * capacity, row_count, block_size), jnp.bfloat16),
            dma((7,)),
            dma((2,)),
            dma((chunks,)),
            dma((chunks,)),
            dma((chunks,)),
            dma((chunks,)),
            dma((1,)),
            dma((1,)),
            dma((capacity,)),
            dma((capacity,)),
            dma((1,)),
            dma((1,)),
            pltpu.SemaphoreType.REGULAR,
            pltpu.SemaphoreType.REGULAR,
        ],
        compiler_params=pltpu.CompilerParams(
            collective_id=0, has_side_effects=True, vmem_limit_bytes=VMEM_UNITS * 2**18
        ),
        name="step",
    )(
        owner_index,
        gradients.reshape(block_count, block_size // unit, unit, block_size),
        left_stats,
        right_stats,
        left_roots,
        right_roots,
        first_moment,
        second_moment,
        master,
    )
    return tuple(
        pl.pallas_call(
            write,
            out_shape=[jax.ShapeDtypeStruct(*leaf) for leaf in shapes],
            in_specs=[vmem] * 5,
            out_specs=[hbm] * 5,
            scratch_shapes=[dma((5,))],
            compiler_params=pltpu.CompilerParams(vmem_limit_bytes=VMEM_UNITS * 2**18),
            name="write",
        )(*[pltpu.with_memory_space_constraint(leaf, pltpu.VMEM) for leaf in results])
    )


def solution(mesh):
    return jax.shard_map(
        functools.partial(local, mesh.shape["rep"], mesh.shape["own"]),
        mesh=mesh,
        in_specs=(
            P("rep", "own", None, None, None),
            P(),
            P("own", None, None),
            P("own", None, None),
            P("own", None, None),
            P("own", None, None),
            P("own", None, None),
            P("own", None, None),
            P("own", None, None),
        ),
        out_specs=(
            P("own", None, None),
            P("own", None, None),
            P("own", None, None),
            P("own", None, None),
            P(None, "rep", None),
        ),
        check_vma=False,
    )
```

```python
import functools

import jax
import jax.numpy as jnp
from jax import lax
from jax.experimental import pallas as pl
from jax.experimental.pallas import tpu as pltpu
from jax.sharding import PartitionSpec as P

NEWTON = 4
VMEM_UNITS = 246


stat_decay = 0.95
first_decay = 0.9
second_decay = 0.99
learning_rate = 0.5


def slot_of(owner_ref, block, capacity):
    rank = jnp.int32(0)
    for earlier in range(block):
        rank = rank + jnp.where(owner_ref[earlier] == owner_ref[block], 1, 0)
    return owner_ref[block] * capacity + rank


def send(source, target, send_sem, recv_sem, device):
    copy = pltpu.make_async_remote_copy(
        src_ref=source,
        dst_ref=target,
        send_sem=send_sem,
        recv_sem=recv_sem,
        device_id=device,
        device_id_type=pl.DeviceIdType.MESH,
    )
    copy.start()
    return copy


def signal(semaphore, device):
    pl.semaphore_signal(
        semaphore, inc=1, device_id=device, device_id_type=pl.DeviceIdType.MESH
    )


def dot(first, second, first_axis=1, second_axis=0):
    return lax.dot_general(
        first,
        second,
        (((first_axis,), (second_axis,)), ((), ())),
        preferred_element_type=jnp.float32,
    )


def parts(value):
    upper = value.astype(jnp.bfloat16)
    lower = (value - upper.astype(jnp.float32)).astype(jnp.bfloat16)
    return upper, lower


def multiply(first, second, first_axis=1, second_axis=0):
    half = first[0].shape[1 - first_axis] // 2
    halves = []
    for rows in (slice(0, half), slice(half, 2 * half)):
        upper, lower = [
            part[rows] if first_axis else part[:, rows] for part in first
        ]
        halves.append(
            dot(upper, second[0], first_axis, second_axis)
            + (
                dot(upper, second[1], first_axis, second_axis)
                + dot(lower, second[0], first_axis, second_axis)
            )
        )
    return jnp.concatenate(halves, axis=0)


def total(value):
    return jnp.sum(jnp.sum(value, axis=0, keepdims=True), axis=1, keepdims=True)


def arrival(target, sem):
    pltpu.make_async_copy(target, target, sem).wait()


def step_kernel(
    reps,
    owns,
    unit,
    pieces,
    owner_in,
    gradients_ref,
    left_ref,
    right_ref,
    left_root_ref,
    right_root_ref,
    first_ref,
    second_ref,
    master_ref,
    new_left_ref,
    new_right_ref,
    new_first_ref,
    new_second_ref,
    weights_ref,
    owner_ref,
    staged,
    raw,
    partial,
    arrived,
    piece_sum,
    summed,
    other,
    roots,
    left_in,
    right_in,
    first_in,
    second_in,
    master_in,
    fifth,
    upper,
    lower,
    current,
    kept,
    outgoing,
    gathered,
    load_sem,
    mine_sem,
    raw_send,
    raw_recv,
    own_send,
    own_recv,
    sum_send,
    sum_recv,
    other_send,
    other_recv,
    row_send,
    row_recv,
    plane_sem,
    ready_sem,
):
    rep = lax.axis_index("rep")
    own = lax.axis_index("own")
    block_count = owner_ref.shape[0]
    capacity = new_left_ref.shape[0]
    block_size = new_left_ref.shape[-1]
    row_count = weights_ref.shape[1]
    units = row_count // unit
    groups = reps // capacity
    high = lax.div(rep, capacity)
    low = lax.rem(rep, capacity)
    sides = range(2)
    chunks = len(pieces)

    def part(chunk, device):
        first, size, column, width = pieces[chunk]
        return pl.ds(device * units + first, size), slice(None), slice(column, column + width)


    def rep_device(target):
        return (target, own)

    def own_device(target):
        return (rep, target)

    pair_rows = pl.ds(
        pl.multiple_of(high * capacity * row_count, capacity * row_count), capacity * row_count
    )
    mine = pltpu.make_async_copy(gradients_ref, staged, mine_sem.at[0])
    mine.start()
    owners = pltpu.make_async_copy(owner_in, owner_ref, mine_sem.at[1])
    owners.start()
    gate, helper = reps - 1, reps - 2
    barrier = pltpu.get_barrier_semaphore()
    for target in range(reps - 1):

        @pl.when(rep != target)
        def _():
            signal(barrier, rep_device(target))

    @pl.when(rep != gate)
    def _():
        pl.semaphore_wait(barrier, reps - 1)

    @pl.when(rep == helper)
    def _():
        signal(plane_sem, rep_device(gate))
        for step in range(1, owns):
            signal(barrier, (gate, lax.rem(own + step, owns)))

    @pl.when(rep == gate)
    def _():
        pl.semaphore_wait(plane_sem, 1)

    mine.wait()
    def flipped_bits(step):
        target = jnp.int32(0)
        for bit in range((reps - 1).bit_length()):
            digit = lax.rem(lax.div(rep, 1 << bit), 2)
            target = target + (1 << bit) * lax.rem(digit + (step >> bit & 1), 2)
        return target

    peers = [
        (step, flipped_bits(step))
        for step in sorted(
            range(1, reps), key=lambda step: (-(step >> 1).bit_count(), -step)
        )
    ]

    def far(turn):
        down = owns - 1 - turn
        down = down - jnp.where(down <= own, 1, 0)
        up = turn + jnp.where(turn >= own, 1, 0)
        return jnp.where(own < owns // 2, down, up)

    for chunk in range(chunks):
        for step, target in peers:
            send(
                staged.at[:, *part(chunk, target)],
                raw[chunk].at[step],
                raw_send.at[chunk],
                raw_recv.at[chunk],
                rep_device(target),
            )
    loads = []
    for place, (source_ref, target_ref) in enumerate(
        (
            (left_root_ref.at[low], roots.at[0]),
            (right_root_ref.at[low], roots.at[1]),
            (left_ref, left_in),
            (right_ref, right_in),
            (first_ref, first_in),
            (second_ref, second_in),
            (master_ref.at[low, pair_rows, :], master_in),
        )
    ):
        loads.append(pltpu.make_async_copy(source_ref, target_ref, load_sem.at[place]))
        loads[-1].start()
    @pl.when(rep == gate)
    def _():
        pl.semaphore_wait(barrier, owns - 1)
        for target in range(reps - 1):
            signal(ready_sem, rep_device(target))

    owners.wait()
    slots = [slot_of(owner_ref, block, capacity) for block in range(block_count)]

    def source(slot):
        found = jnp.int32(0)
        for block in range(block_count):
            found = found + jnp.where(slots[block] == slot, block, 0)
        return found

    loads[0].wait()
    loads[1].wait()
    squares = [parts(dot(roots[side], roots[side])) for side in sides]
    fourths = [parts(multiply(squares[side], squares[side])) for side in sides]
    for side in sides:
        fifth[side] = dot(roots[side], fourths[side][0]) + dot(roots[side], fourths[side][1])

    for chunk in range(chunks):
        arrival(raw[chunk].at[1:reps], raw_recv.at[chunk])
        if chunk == 0:

            @pl.when(rep != gate)
            def _():
                pl.semaphore_wait(ready_sem, 1)

        for turn in range(owns):
            target = far(turn) if turn < owns - 1 else own
            step = lax.rem(target - own + owns, owns) if turn < owns - 1 else 0
            for place in range(capacity):
                block = source(target * capacity + place)
                value = staged[block, *part(chunk, rep)].astype(jnp.float32)
                for peer in range(1, reps):
                    value = value + raw[chunk][peer, block].astype(jnp.float32)
                partial[chunk][step, place] = value.reshape(
                    partial[chunk].shape[2:]
                )
            if turn < owns - 1:
                send(
                    partial[chunk].at[step],
                    arrived[chunk].at[step],
                    own_send.at[chunk],
                    own_recv.at[chunk],
                    own_device(target),
                )

    for chunk in range(chunks):
        arrival(arrived[chunk].at[1:owns], own_recv.at[chunk])
        value = partial[chunk][0]
        for step in range(1, owns):
            value = value + arrived[chunk][step]
        piece_sum[chunk][...] = value
        first, size, column, width = pieces[chunk]
        start = pl.multiple_of(rep * row_count + first * unit, unit)
        rows, columns = pl.ds(start, size * unit), slice(column, column + width)
        for step, target in peers:
            send(
                piece_sum[chunk].at[lax.rem(target, capacity)],
                summed.at[rows, columns],
                sum_send.at[0],
                sum_recv.at[0],
                rep_device(target),
            )
        summed[rows, columns] = piece_sum[chunk][low]
    for copy in loads[2:]:
        copy.wait()
    arrival(summed.at[0 : block_size - row_count], sum_recv.at[0])
    others = [
        send(
            summed,
            other.at[step],
            other_send.at[step],
            other_recv.at[step],
            rep_device(high * capacity + lax.rem(low + step, capacity)),
        )
        for step in range(1, capacity)
    ]

    scale = (1.0 - stat_decay) / block_size

    def occupied(place):
        count = jnp.int32(0)
        for block in range(block_count):
            count = count + jnp.where(slots[block] == own * capacity + place, 1, 0)
        return count > 0

    def moments(place, gradient, held):
        first_new = first_decay * first_in[place] + (1.0 - first_decay) * gradient
        second_new = (
            second_decay * second_in[place] + (1.0 - second_decay) * gradient * gradient
        )
        new_first_ref[place] = jnp.where(held, first_new, first_in[place])
        new_second_ref[place] = jnp.where(held, second_new, second_in[place])
        return first_new, second_new

    def statistics(place, gradient, held):
        split, flipped = parts(gradient), parts(gradient.T)
        left = stat_decay * left_in[place] + scale * multiply(split, flipped)
        right = stat_decay * right_in[place] + scale * multiply(flipped, split)
        new_left_ref[place] = jnp.where(held, left, left_in[place])
        new_right_ref[place] = jnp.where(held, right, right_in[place])
        return left, right

    held = occupied(low)
    gradient = summed[...]
    for side, value in enumerate(statistics(low, gradient, held)):
        upper[side], lower[side] = parts(value)

    def statistic(side):
        return upper[side], lower[side]

    for side in sides:
        current[side] = (
            5.0 * roots[side].astype(jnp.float32)
            - multiply(parts(fifth[side]), statistic(side))
        ) / 4.0
    first_new, second_new = moments(low, gradient, held)
    adam_step = first_new / (jnp.sqrt(second_new) + 1e-08)
    adam_norm = jnp.sqrt(total(adam_step * adam_step))

    def newton(iteration, carry):
        split = [parts(current[side]) for side in sides]
        squares = [parts(multiply(split[side], split[side])) for side in sides]
        rests = [parts(multiply(squares[side], statistic(side))) for side in sides]
        cubes = [parts(multiply(split[side], squares[side])) for side in sides]
        for side in sides:
            current[side] = 1.25 * current[side] - 0.25 * multiply(cubes[side], rests[side])
        return carry

    for iteration in range(1, NEWTON):
        newton(iteration, 0)

    halfway = multiply(parts(current[0]), parts(summed[...]))
    precond = multiply(parts(halfway), parts(current[1]))
    graft = adam_norm / (jnp.sqrt(total(precond * precond)) + 1e-06)
    kept[...] = precond
    weight = (master_in[...] - learning_rate * graft * kept[pair_rows, :]).astype(jnp.bfloat16)
    for member in range(capacity):
        outgoing[member] = weight[member * row_count : (member + 1) * row_count]
    for turn in range(owns):
        target = far(turn) if turn < owns - 1 else own
        step = lax.rem(target - own + owns, owns) if turn < owns - 1 else 0
        for shift in range(capacity):
            if turn < owns - 1 or shift:
                member = lax.rem(low + shift, capacity)
                send(
                    outgoing.at[member],
                    gathered.at[step * capacity + low],
                    row_send.at[0],
                    row_recv.at[0],
                    (high * capacity + member, target),
                )
    gathered[low] = outgoing[low]

    for step in range(1, capacity):
        others[step - 1].wait_recv()
        place = lax.rem(low + capacity - step, capacity)
        gradient = other[step]
        held = occupied(place)
        statistics(place, gradient, held)
        moments(place, gradient, held)
    for chunk in range(chunks):
        arrival(raw[chunk].at[1:reps], raw_send.at[chunk])
        arrival(arrived[chunk].at[1:owns], own_send.at[chunk])
    arrival(summed.at[0 : block_size - row_count], sum_send.at[0])
    for copy in others:
        copy.wait_send()
    arrival(gathered.at[1 : owns * capacity], row_send.at[0])
    arrival(gathered.at[1 : owns * capacity], row_recv.at[0])
    for block in range(block_count):
        step = lax.rem(own + owns - owner_ref[block], owns)
        place = jnp.minimum(slots[block] - owner_ref[block] * capacity, capacity - 1)
        weights_ref[block] = gathered[step * capacity + place]


def write(*refs):
    count = (len(refs) - 1) // 2
    stores = []
    for index in range(count):
        source_ref, target_ref = refs[index], refs[count + index]
        stores.append(pltpu.make_async_copy(source_ref, target_ref, refs[-1].at[index]))
        stores[-1].start()
    for store in stores:
        store.wait()


def local(
    reps,
    owns,
    gradients,
    owner_index,
    left_stats,
    right_stats,
    left_roots,
    right_roots,
    first_moment,
    second_moment,
    master,
):
    capacity = left_stats.shape[0]
    block_size = left_stats.shape[-1]
    block_count = owner_index.shape[0]
    row_count = block_size // reps
    unit = 8
    units = row_count // unit
    half = block_size // 2
    pieces = [(first, 1, 0, block_size) for first in range(units - 1)]
    pieces += [(units - 1, 1, column, half) for column in (0, half)]
    chunks = len(pieces)
    vmem = pl.BlockSpec(memory_space=pltpu.VMEM)
    hbm = pl.BlockSpec(memory_space=pltpu.HBM)
    dma = pltpu.SemaphoreType.DMA
    square = (block_size, block_size)
    piece_shapes = [(capacity, size * unit, width) for _, size, _, width in pieces]
    whole = (capacity, *square)
    double = (2, *square)
    shapes = [(whole, jnp.float32)] * 4 + [((block_count, row_count, block_size), jnp.bfloat16)]

    results = pl.pallas_call(
        functools.partial(step_kernel, reps, owns, unit, pieces),
        out_shape=[pltpu.VMEM(*leaf) for leaf in shapes],
        in_specs=[hbm] * 9,
        out_specs=[vmem] * 5,
        scratch_shapes=[
            pltpu.SMEM((block_count,), jnp.int32),
            pltpu.VMEM((block_count, block_size // unit, unit, block_size), jnp.bfloat16),
            tuple(
                pltpu.VMEM((reps, block_count, size, unit, width), jnp.bfloat16)
                for _, size, _, width in pieces
            ),
            tuple(pltpu.VMEM((owns, *piece), jnp.float32) for piece in piece_shapes),
            tuple(pltpu.VMEM((owns, *piece), jnp.float32) for piece in piece_shapes),
            tuple(pltpu.VMEM(piece, jnp.float32) for piece in piece_shapes),
            pltpu.VMEM(square, jnp.float32),
            pltpu.VMEM(whole, jnp.float32),
            pltpu.VMEM(double, jnp.bfloat16),
            pltpu.VMEM(whole, jnp.float32),
            pltpu.VMEM(whole, jnp.float32),
            pltpu.VMEM(whole, jnp.float32),
            pltpu.VMEM(whole, jnp.float32),
            pltpu.VMEM((capacity * row_count, block_size), jnp.float32),
            pltpu.VMEM(double, jnp.float32),
            pltpu.VMEM(double, jnp.bfloat16),
            pltpu.VMEM(double, jnp.bfloat16),
            pltpu.VMEM(double, jnp.float32),
            pltpu.VMEM(square, jnp.float32),
            pltpu.VMEM((capacity, row_count, block_size), jnp.bfloat16),
            pltpu.VMEM((owns * capacity, row_count, block_size), jnp.bfloat16),
            dma((7,)),
            dma((2,)),
            dma((chunks,)),
            dma((chunks,)),
            dma((chunks,)),
            dma((chunks,)),
            dma((1,)),
            dma((1,)),
            dma((capacity,)),
            dma((capacity,)),
            dma((1,)),
            dma((1,)),
            pltpu.SemaphoreType.REGULAR,
            pltpu.SemaphoreType.REGULAR,
        ],
        compiler_params=pltpu.CompilerParams(
            collective_id=0, has_side_effects=True, vmem_limit_bytes=VMEM_UNITS * 2**18
        ),
        name="step",
    )(
        owner_index,
        gradients.reshape(block_count, block_size // unit, unit, block_size),
        left_stats,
        right_stats,
        left_roots,
        right_roots,
        first_moment,
        second_moment,
        master,
    )
    return tuple(
        pl.pallas_call(
            write,
            out_shape=[jax.ShapeDtypeStruct(*leaf) for leaf in shapes],
            in_specs=[vmem] * 5,
            out_specs=[hbm] * 5,
            scratch_shapes=[dma((5,))],
            compiler_params=pltpu.CompilerParams(vmem_limit_bytes=VMEM_UNITS * 2**18),
            name="write",
        )(*[pltpu.with_memory_space_constraint(leaf, pltpu.VMEM) for leaf in results])
    )


def solution(mesh):
    return jax.shard_map(
        functools.partial(local, mesh.shape["rep"], mesh.shape["own"]),
        mesh=mesh,
        in_specs=(
            P("rep", "own", None, None, None),
            P(),
            P("own", None, None),
            P("own", None, None),
            P("own", None, None),
            P("own", None, None),
            P("own", None, None),
            P("own", None, None),
            P("own", None, None),
        ),
        out_specs=(
            P("own", None, None),
            P("own", None, None),
            P("own", None, None),
            P("own", None, None),
            P(None, "rep", None),
        ),
        check_vma=False,
    )
```
